1024 devices in a mesh: seq: 32 (over y, z_lo), tp: 32 (over z_hi, x, core).
Axes of the slice: x: 8, y: 8, z: 8 (z_hi: 2, z_lo: 4; z = z_hi * 4 + z_lo), core: 2. Of those that a mesh axis runs over, the one named last changes fastest.
Arguments:
- lin_query: bfloat16 [8192, 64, 128], P('seq', 'tp'), may hold values from -6 to 6
- lin_key: bfloat16 [8192, 64, 128], P('seq', 'tp'), may hold values from -6 to 6
- lin_value: bfloat16 [8192, 64, 128], P('seq', 'tp'), may hold values from -80 to 80
- lin_gate: bfloat16 [8192, 64, 128], P('seq', 'tp'), may hold values from -6 to 6
- log_decay: float32 [8192, 64], P('seq', 'tp'), may hold values from -1 to 0
- norm_gain: float32 [64, 128], P('tp'), may hold values from 0.1 to 1.9
- doc_ids: int32 [8192], P('seq'), may hold values from 0 to 3, never falling along the last dimension, each value on 1 to 5120 neighbouring positions
- soft_query: bfloat16 [8192, 64, 128], P('seq', 'tp'), may hold values from -200 to 200
- soft_key: bfloat16 [8192, 8, 128], P('seq'), may hold values from -6 to 6
- soft_value: bfloat16 [8192, 8, 128], P('seq'), may hold values from -6 to 6
Outputs:
- lin_out: bfloat16 [8192, 64, 128], P('seq', 'tp')
- soft_out: bfloat16 [8192, 64, 128], P('seq', 'tp')
The draws below stay inside these ranges and needn't reach their ends.
Inputs may be any that keep to these rules, and one draw needn't show every extreme that they name: `doc_ids`: ids never fall along the sequence; each document is one run of 1 to 5120 tokens, and one document has exactly that many.
All inputs are finite; a program needn't handle non-finite values.
Results may differ from the reference program's by a relative error of at most 0.012.
Values may be sent and summed in bfloat16 or wider, within the bound.
A program may use at most 32 MiB of HBM per device.

```python
import math
import jax
import jax.numpy as jnp
import numpy as np
from jax import lax

HEADS = 64
HEAD_DIM = 128
KV_HEADS = 8
TOK_DEV = 256
DOCS = 4
STREAM_LENGTH = 8192


def draw_lin_value(key, part):
    base_key = jax.random.fold_in(key, 21)
    spread_key = jax.random.fold_in(key, 22)
    shape = (STREAM_LENGTH, HEADS, HEAD_DIM)
    base = jnp.clip(jax.random.normal(base_key, shape, jnp.float32), -6.0, 6.0)
    top_ramp = 3.0
    ramp = jnp.exp(math.log(top_ramp) * jnp.arange(HEADS).astype(jnp.float32) / (HEADS - 1))
    spread = jnp.exp(jax.random.uniform(spread_key, (HEADS,), jnp.float32, math.log(0.7), math.log(1.4)))
    return (base * (ramp * spread)[None, :, None]).astype(jnp.bfloat16)


def draw_log_decay(key, part):
    share_key = jax.random.fold_in(key, 31)
    slow_key = jax.random.fold_in(key, 32)
    fast_key = jax.random.fold_in(key, 33)
    block_key = jax.random.fold_in(key, 34)
    spike_seed = jax.random.fold_in(key, 35)
    keep_key = jax.random.fold_in(key, 36)
    share = 0.5
    slow_heads = jax.random.uniform(share_key, (HEADS,), jnp.float32) < share
    slow_rate = 0.25 * math.log(10.0) / STREAM_LENGTH * jnp.exp(jax.random.uniform(slow_key, (HEADS,), jnp.float32, math.log(0.2), 0.0))
    fast_rate = jnp.exp(jax.random.uniform(fast_key, (HEADS,), jnp.float32, math.log(1.0 / 50.0), math.log(1.0 / 30.0)))
    rate = jnp.where(slow_heads, slow_rate, fast_rate)
    block_count = STREAM_LENGTH // TOK_DEV
    block_factor = jnp.exp(jax.random.uniform(block_key, (block_count, HEADS), jnp.float32, -0.69, 0.69))
    block_factor = jnp.repeat(block_factor, TOK_DEV, axis=0)
    shrink_multiplier = -rate[None, :] * block_factor
    spike_offset = jax.random.randint(spike_seed, (2,), 0, STREAM_LENGTH)
    word_offsets = jnp.arange(STREAM_LENGTH)
    word_spike = jnp.any(word_offsets[:, None] == spike_offset[None, :], axis=1)
    retained_ratio = jax.random.uniform(keep_key, (STREAM_LENGTH, HEADS), jnp.float32, 0.6, 0.8)
    shrink_multiplier = shrink_multiplier + jnp.where(word_spike[:, None], jnp.log(retained_ratio), 0.0)
    return shrink_multiplier.astype(jnp.float32)


def soft_pair(key):
    key_draw = jax.random.fold_in(key, 11)
    query_draw = jax.random.fold_in(key, 12)
    key_rows = jnp.clip(jax.random.normal(key_draw, (STREAM_LENGTH, KV_HEADS, HEAD_DIM), jnp.float32), -6.0, 6.0)
    query_rows = jnp.clip(jax.random.normal(query_draw, (STREAM_LENGTH, HEADS, HEAD_DIM), jnp.float32), -6.0, 6.0)
    return (query_rows, key_rows)


def draw_soft_query(key, part):
    return soft_pair(key)[0].astype(jnp.bfloat16)


def draw_soft_key(key, part):
    return soft_pair(key)[1].astype(jnp.bfloat16)


def shard_levels(own_key, dims, cuts, least, high):
    loudness = 1.0
    for dim, shards_of in cuts:
        heights = jax.random.uniform(jax.random.fold_in(jax.random.fold_in(own_key, 6), dim), (shards_of,), jnp.float32, least / len(cuts), high / len(cuts))
        loudness = loudness * jnp.repeat(jnp.exp(heights), dims[dim] // shards_of).reshape((-1,) + (1,) * (len(dims) - 1 - dim))
    return loudness


def length_profile(number_of, total, limit, skew):
    loads = [(1 << 20) // math.isqrt(standing ** skew) + 1 for standing in range(2, number_of + 1)]
    surplus, given = total - limit - (number_of - 1), [1] * (number_of - 1)
    while surplus > 0:
        movable = [i for i in range(number_of - 1) if given[i] < limit]
        mass, left = sum([loads[i] for i in movable]), surplus
        for i in movable:
            extra = min(limit - given[i], max(1, left * loads[i] // mass), surplus)
            given[i] = given[i] + extra
            surplus = surplus - extra
    return np.array([limit] + given)


def uneven(own_key, number_of, total, most, slope):
    if number_of == 2:
        one = jax.random.randint(own_key, (), max(1, total - most), min(most, total - 1) + 1)
        return jnp.stack([one, total - one])
    lengths = jnp.asarray(length_profile(number_of, total, most, slope), jnp.int32)
    twos = (number_of - 1) // 2
    source_of, taker = lengths[1:1 + 2 * twos:2], lengths[2:2 + 2 * twos:2]
    room = jnp.minimum(source_of - 1, most - taker)
    moved = jax.random.randint(jax.random.fold_in(own_key, 1), (twos,), 0, 1 << 20) % (room + 1)
    lengths = lengths.at[1:1 + 2 * twos:2].set(source_of - moved).at[2:2 + 2 * twos:2].set(taker + moved)
    return lengths[jax.random.permutation(jax.random.fold_in(own_key, 2), number_of)]


def scatter_about(key, shape, scale, limit, cuts=(), held_as=jnp.bfloat16):
    values = scale * jax.random.normal(key, shape, jnp.float32)
    if cuts:
        values = values * shard_levels(key, shape, cuts, -0.22, 0.18)
    return jnp.clip(values, -limit, limit).astype(held_as)


def setup_inputs(seed: int = 0) -> dict:
    keys = jax.random.split(jax.random.key(seed), 11)
    return {
        "lin_query": scatter_about(keys[0], (STREAM_LENGTH, HEADS, HEAD_DIM), 1.0, 6.0, ((0, 32), (1, 32))),
        "lin_key": scatter_about(keys[1], (STREAM_LENGTH, HEADS, HEAD_DIM), 1.0, 6.0, ((0, 32), (1, 32))),
        "lin_value": draw_lin_value(jax.random.fold_in(keys[10], 71), 0),
        "lin_gate": scatter_about(keys[3], (STREAM_LENGTH, HEADS, HEAD_DIM), 1.5, 6.0, ((0, 32), (1, 32))),
        "log_decay": draw_log_decay(jax.random.fold_in(keys[10], 71), 0),
        "norm_gain": jnp.clip(1.0 + 0.18 * jax.random.normal(keys[5], (HEADS, HEAD_DIM), jnp.float32), 0.1, 1.9),
        "doc_ids": jnp.searchsorted(jnp.cumsum(uneven(keys[6], DOCS, STREAM_LENGTH, STREAM_LENGTH * 5 // 8, 0)), jnp.arange(STREAM_LENGTH), side="right").astype(jnp.int32),
        "soft_query": draw_soft_query(jax.random.fold_in(keys[10], 71), 0),
        "soft_key": draw_soft_key(jax.random.fold_in(keys[10], 71), 0),
        "soft_value": scatter_about(keys[9], (STREAM_LENGTH, KV_HEADS, HEAD_DIM), 1.0, 6.0, ((0, 32),)),
    }


def lightning_reference(lin_query, lin_key, lin_value, lin_gate, log_decay, norm_gain, doc_ids):
    block_count = STREAM_LENGTH // TOK_DEV
    query_blocks = lin_query.reshape(block_count, TOK_DEV, HEADS, HEAD_DIM)
    key_blocks = lin_key.reshape(block_count, TOK_DEV, HEADS, HEAD_DIM)
    value_blocks = lin_value.reshape(block_count, TOK_DEV, HEADS, HEAD_DIM)
    decay_blocks = log_decay.reshape(block_count, TOK_DEV, HEADS)
    doc_blocks = doc_ids.reshape(block_count, TOK_DEV)
    token_order = jnp.arange(TOK_DEV).astype(jnp.int32)
    highest = lax.Precision.HIGHEST

    def advance(running, block_data):
        prior_state, prior_doc = running
        query, key_rows, value_rows, shrink_multiplier, block_docs = block_data
        cumul = jnp.cumsum(shrink_multiplier, axis=0)
        visible = (token_order[None, :] <= token_order[:, None]) & (block_docs[None, :] == block_docs[:, None])
        cumul_heads = jnp.transpose(cumul)
        decay_gap = cumul_heads[:, :, None] - cumul_heads[:, None, :]
        factor = jnp.where(visible[None], jnp.exp(jnp.where(visible[None], decay_gap, 0.0)), 0.0)
        scores = jnp.einsum('thd,shd->hts', query.astype(jnp.float32), key_rows.astype(jnp.float32), precision=highest)
        weights = lax.optimization_barrier((scores * factor).astype(jnp.bfloat16))
        inner_part = jnp.einsum('hts,shd->thd', weights.astype(jnp.float32), value_rows.astype(jnp.float32), precision=highest)
        tail_mask = (block_docs == block_docs[-1]).astype(jnp.float32)
        key_scale = jnp.exp(cumul[-1][None, :] - cumul) * tail_mask[:, None]
        scaled_keys = lax.optimization_barrier((key_rows.astype(jnp.float32) * key_scale[:, :, None]).astype(jnp.bfloat16))
        block_state = jnp.einsum('shd,she->hde', scaled_keys.astype(jnp.float32), value_rows.astype(jnp.float32), precision=highest)
        state_rounded = lax.optimization_barrier(prior_state.astype(jnp.bfloat16))
        carried = jnp.einsum('thd,hde->the', query.astype(jnp.float32), state_rounded.astype(jnp.float32), precision=highest)
        open_mask = (block_docs == prior_doc).astype(jnp.float32)
        carried = carried * (jnp.exp(cumul) * open_mask[:, None])[:, :, None]
        linked = (prior_doc == block_docs[0]) & (block_docs[0] == block_docs[-1])
        passed = jnp.where(linked, jnp.exp(cumul[-1]), 0.0)
        next_state = passed[:, None, None] * prior_state + block_state
        return ((next_state, block_docs[-1]), inner_part + carried)
    start_state = jnp.zeros((HEADS, HEAD_DIM, HEAD_DIM), jnp.float32)
    start_doc = jnp.array(-1, dtype=doc_ids.dtype)
    _, mixed_blocks = lax.scan(advance, (start_state, start_doc), (query_blocks, key_blocks, value_blocks, decay_blocks, doc_blocks))
    mixed_heads = mixed_blocks.reshape(STREAM_LENGTH, HEADS, HEAD_DIM)
    square_mean = lax.optimization_barrier(jnp.mean(mixed_heads * mixed_heads, axis=(1, 2)))
    inv_rms = lax.rsqrt(square_mean + 1e-06)
    gated = jax.nn.sigmoid(lin_gate.astype(jnp.float32))
    return (mixed_heads * inv_rms[:, None, None] * norm_gain[None] * gated).astype(jnp.bfloat16)

def softmax_reference(soft_query, soft_key, soft_value, doc_ids):
    group_size = HEADS // KV_HEADS
    block_count = STREAM_LENGTH // TOK_DEV
    word_offsets = jnp.arange(STREAM_LENGTH).astype(jnp.int32)
    keys_by_head = jnp.transpose(soft_key, (1, 0, 2)).astype(jnp.float32)
    values_by_head = jnp.transpose(soft_value, (1, 0, 2)).astype(jnp.float32)
    query_blocks = soft_query.reshape(block_count, TOK_DEV, KV_HEADS, group_size, HEAD_DIM)
    score_scale = HEAD_DIM ** (-0.5)
    highest = lax.Precision.HIGHEST

    def one_block(block_index):
        query = lax.dynamic_index_in_dim(query_blocks, block_index, 0, keepdims=False)
        first_row = (block_index * TOK_DEV).astype(jnp.int32)
        query_pos = first_row + jnp.arange(TOK_DEV).astype(jnp.int32)
        query_docs = lax.dynamic_slice_in_dim(doc_ids, first_row, TOK_DEV)
        visible = (word_offsets[None, :] <= query_pos[:, None]) & (doc_ids[None, :] == query_docs[:, None])

        def one_head(head_index):
            head_query = lax.dynamic_index_in_dim(query, head_index, 1, keepdims=False).astype(jnp.float32)
            head_keys = lax.dynamic_index_in_dim(keys_by_head, head_index, 0, keepdims=False)
            head_values = lax.dynamic_index_in_dim(values_by_head, head_index, 0, keepdims=False)
            score = jnp.einsum('tgd,sd->gts', head_query, head_keys, precision=highest) * score_scale
            score = jnp.where(visible[None], score, -1e+30)
            top_score = lax.optimization_barrier(jnp.max(score, axis=-1, keepdims=True))
            soft_exp = jnp.where(visible[None], jnp.exp(score - top_score), 0.0)
            soft_total = lax.optimization_barrier(jnp.sum(soft_exp, axis=-1))
            soft_weights = lax.optimization_barrier(soft_exp.astype(jnp.bfloat16))
            weighted = jnp.einsum('gts,sd->gtd', soft_weights.astype(jnp.float32), head_values, precision=highest)
            return (weighted / soft_total[..., None]).astype(jnp.bfloat16)
        per_head = lax.map(one_head, jnp.arange(KV_HEADS).astype(jnp.int32))
        return jnp.transpose(per_head, (2, 0, 1, 3)).reshape(TOK_DEV, HEADS, HEAD_DIM)
    result = lax.map(one_block, jnp.arange(block_count).astype(jnp.int32))
    return result.reshape(STREAM_LENGTH, HEADS, HEAD_DIM)

def reference(lin_query, lin_key, lin_value, lin_gate, log_decay, norm_gain, doc_ids, soft_query, soft_key, soft_value):
    lin_out = lightning_reference(lin_query, lin_key, lin_value, lin_gate, log_decay, norm_gain, doc_ids)
    soft_out = softmax_reference(soft_query, soft_key, soft_value, doc_ids)
    return (lin_out, soft_out)
```

```python
import functools

import jax
import jax.numpy as jnp
from jax import lax
from jax.experimental import pallas as pl
from jax.experimental.pallas import tpu as pltpu
from jax.sharding import Mesh
from jax.sharding import PartitionSpec as P

HEADS = 64
HEAD_DIM = 128
KV_HEADS = 8
SEQ = ("y", "z")
TP = ("w", "x", "c")
MESH = pl.DeviceIdType.MESH
F32 = jnp.float32
BF16 = jnp.bfloat16
BACK = 5
LOW = -1e30


def dot_nt(a, b, **kw):
    return lax.dot_general(a, b, (((1,), (1,)), ((), ())), preferred_element_type=F32, **kw)


def dot_tn(a, b):
    return lax.dot_general(a, b, (((0,), (0,)), ((), ())), preferred_element_type=F32)


def dot_nn(a, b):
    return lax.dot_general(a, b, (((1,), (0,)), ((), ())), preferred_element_type=F32)


def as_column(row, toks):
    return jnp.concatenate(
        [
            jnp.transpose(jnp.broadcast_to(row[:, k : k + 128], (128, 128)))
            for k in range(0, toks, 128)
        ],
        axis=0,
    )


def three_parts(line):
    high = line.astype(BF16)
    rest = line - high.astype(F32)
    middle = rest.astype(BF16)
    low = (rest - middle.astype(F32)).astype(BF16)
    row = lax.broadcasted_iota(jnp.int32, (16, 128), 0)
    parts = [jnp.broadcast_to(p.astype(F32), (16, 128)) for p in (high, middle, low)]
    return jnp.where(
        row == 0, parts[0], jnp.where(row == 1, parts[1], jnp.where(row == 2, parts[2], 0.0))
    ).astype(BF16)


def from_parts(tile):
    wide = tile.astype(F32)
    return wide[0:1] + wide[1:2] + wide[2:3]


def kernel(
    sizes,
    lq,
    lk,
    lv,
    lg,
    ld,
    gain,
    docs,
    sq,
    sk,
    sv,
    lin_out,
    soft_out,
    kv,
    wide8,
    wq,
    wk,
    wv,
    wg,
    wo,
    dec,
    ccol,
    dcol,
    dq,
    mix,
    s_out,
    s_in,
    t_out,
    t_in,
    p_out,
    p_in,
    run_state,
    run_decay,
    pdoc,
    ss_in,
    m_scr,
    l_scr,
    acc,
    p_sem,
    x_sem,
    c_sem,
    s_sem,
    t_sem,
    st_sem,
    ss_sem,
    za_snd,
    a_snd,
    a5_snd,
    b_snd,
    x_snd,
    s_snd,
    t_snd,
    p_snd,
    ss_snd,
):
    n_y, n_z, n_w, n_x, n_c = sizes
    n_tp = n_w * n_x * n_c
    toks = lq.shape[0] // 2
    y, z, w = (lax.axis_index("y"), lax.axis_index("z"), lax.axis_index("w"))
    x, c = (lax.axis_index("x"), lax.axis_index("c"))
    tp = (w * n_x + x) * n_c + c
    half = lax.rem(x, 2)
    other_half = 1 - half
    x_mate = x + 1 - 2 * half
    c_mate = 1 - c
    head = (tp * 2) // (HEADS // KV_HEADS)

    def tp_place(k):
        t2 = lax.rem(tp + k, n_tp)
        return {"w": t2 // (n_x * n_c), "x": lax.rem(t2 // n_c, n_x), "c": lax.rem(t2, n_c)}

    barrier = pltpu.get_barrier_semaphore()

    def greet_tp(k, carry):
        pl.semaphore_signal(barrier, inc=1, device_id=tp_place(k), device_id_type=MESH)
        return carry

    def greet_y(k, carry):
        pl.semaphore_signal(
            barrier, inc=1, device_id={"y": lax.rem(y + k, n_y)}, device_id_type=MESH
        )
        return carry

    for k in range(1, n_z):
        pl.semaphore_signal(
            barrier, inc=1, device_id={"z": lax.rem(z + k, n_z)}, device_id_type=MESH
        )
    lax.fori_loop(1, n_y, greet_y, 0)
    lax.fori_loop(1, n_tp, greet_tp, 0)

    def send(src, dst, send_sem, recv_sem, device):
        pltpu.make_async_remote_copy(
            src_ref=src,
            dst_ref=dst,
            send_sem=send_sem,
            recv_sem=recv_sem,
            device_id=device,
            device_id_type=MESH,
        ).start()

    def landed(ref, sem):
        pltpu.make_async_remote_copy(
            src_ref=ref,
            dst_ref=ref,
            send_sem=a5_snd.at[0],
            recv_sem=sem,
            device_id={"c": c_mate},
            device_id_type=MESH,
        ).wait_recv()

    def left(ref, sem):
        pltpu.make_async_remote_copy(
            src_ref=ref,
            dst_ref=ref,
            send_sem=sem,
            recv_sem=p_sem.at[0],
            device_id={"c": c_mate},
            device_id_type=MESH,
        ).wait_send()

    doc_row = docs[...].astype(F32)
    pack_row = lax.broadcasted_iota(jnp.int32, (16, 128), 0)
    doc_tile = jnp.zeros((16, 128), F32)
    for k in range(toks // 128):
        piece = jnp.broadcast_to(doc_row[:, 128 * k : 128 * (k + 1)], (16, 128))
        doc_tile = jnp.where(pack_row == k, piece, doc_tile)
    doc_tile = doc_tile.astype(BF16)
    for kind, source in ((0, sk), (1, sv)):
        wide8[kind] = source[...].astype(F32)
        kv[kind, z, 0:toks, :] = wide8[kind, pl.ds(head, toks, stride=KV_HEADS), :].astype(BF16)
        kv[kind, z, toks : toks + 16, :] = doc_tile

    doc_col = as_column(doc_row, toks)
    dcol[...] = doc_col
    for h in range(2):
        dq[pl.ds(h, toks, stride=2), :] = doc_col
    for source, target in ((lq, wq), (lk, wk), (lv, wv), (lg, wg)):
        target[...] = source[...].astype(F32)

    dec[...] = jnp.zeros_like(dec)
    dec[0:2, :] = ld[...]
    t_id = lax.broadcasted_iota(jnp.int32, (toks, toks), 0)
    s_id = lax.broadcasted_iota(jnp.int32, (toks, toks), 1)
    upto = (s_id <= t_id).astype(F32)
    cum_col = dot_nt(upto, dec[...], precision=lax.Precision.HIGHEST)
    cum_row = dot_nt(dec[...], upto, precision=lax.Precision.HIGHEST)
    ccol[...] = cum_col
    last_doc = doc_row[:, toks - 1 : toks]
    tail = (doc_col[:, :1] == last_doc).astype(F32)
    queries = [wq[pl.ds(h, toks, stride=2), :].astype(BF16) for h in range(2)]
    keys = [wk[pl.ds(h, toks, stride=2), :] for h in range(2)]
    values = [wv[pl.ds(h, toks, stride=2), :].astype(BF16) for h in range(2)]
    decay_line = jnp.zeros((1, 128), F32)
    lane = lax.broadcasted_iota(jnp.int32, (1, 128), 1)
    for h in range(2):
        end = cum_col[toks - 1 : toks, h : h + 1]
        scale = jnp.exp(end - cum_col[:, h : h + 1]) * tail
        state = dot_tn((keys[h] * scale).astype(BF16), values[h]).astype(BF16)
        for q in range(4):
            s_out[q, 32 * h : 32 * h + 32, :] = state[32 * q : 32 * q + 32, :]
        decay_line = jnp.where(lane == h, end, decay_line)
    decay_line = jnp.where(lane == 2, last_doc, decay_line)
    scalars = three_parts(decay_line)
    for q in range(4):
        s_out[q, 64:80, :] = scalars
    s_in[z] = s_out[z]
    visible = (s_id <= t_id) & (doc_row == doc_col[:, :1])
    for h in range(2):
        gap = cum_col[:, h : h + 1] - cum_row[h : h + 1, :]
        factor = jnp.where(visible, jnp.exp(jnp.where(visible, gap, 0.0)), 0.0)
        weights = (dot_nt(queries[h], keys[h].astype(BF16)) * factor).astype(BF16)
        mix[h] = dot_nn(weights, values[h])
    m_scr[...] = jnp.full_like(m_scr, LOW)
    l_scr[...] = jnp.zeros_like(l_scr)
    acc[...] = jnp.zeros_like(acc)

    pl.semaphore_wait(barrier, (n_z - 1) + (n_y - 1) + (n_tp - 1))

    for k in range(1, n_z):
        z2 = lax.rem(z + k, n_z)
        send(s_out.at[z2], s_in.at[z], s_snd.at[k - 1], s_sem.at[z], {"z": z2})
    owner = ((z == 0) | (z == 3)) == (half == 0)

    @pl.when(owner)
    def _():
        for k in range(1, n_z):
            z2 = lax.rem(z + k, n_z)
            send(kv.at[c, z], kv.at[c, z], za_snd.at[k - 1], p_sem.at[z // 2], {"z": z2})

    for k in range(1, n_z):
        z2 = lax.rem(z + k, n_z)
        landed(s_in.at[z2], s_sem.at[z2])
    lines = [from_parts(s_in[k, 64:80, :]) for k in range(4)]
    ends = [line[:, 2:3] for line in lines]

    def weight_of(first, last, h, doc):
        total = jnp.zeros((1, 1), F32)
        for k in range(first, last + 1):
            total = total + lines[k][:, h : h + 1]
        return jnp.where(doc == ends[last], jnp.exp(total), 0.0)

    total_line = lines[0] + lines[1] + lines[2] + lines[3]
    for h in range(2):
        rows = slice(32 * h, 32 * h + 32)
        total = s_in[3, rows, :].astype(F32)
        for k in range(3):
            total = total + s_in[k, rows, :].astype(F32) * weight_of(k + 1, 3, h, ends[k])
        t_out[rows, :] = total.astype(BF16)
    t_out[64:80, :] = three_parts(jnp.where(lane == 2, ends[3], total_line))
    for d in range(1, BACK + 1):

        @pl.when(y + d < n_y)
        def _(d=d):
            send(t_out, t_in.at[d], t_snd.at[d], t_sem.at[d], {"y": y + d})

    def place(which, j):
        return which + j * (3 - 2 * which)

    def primary(d):
        for j in range(2):
            zz = place(half, j)
            unit = kv.at[c, 4 * d + zz]
            mine = (d == 0) & (zz == z)

            @pl.when(jnp.logical_not(mine))
            def _():
                landed(unit, p_sem.at[2 * d + j])

            @pl.when((y + 1 < n_y) & (d + 1 < BACK))
            def _():
                send(
                    unit,
                    kv.at[c, 4 * d + 4 + zz],
                    a_snd.at[2 * d + j],
                    p_sem.at[2 * d + 2 + j],
                    {"y": lax.rem(y + 1, n_y)},
                )

            @pl.when((y + BACK < n_y) & (d == 0))
            def _():
                send(
                    unit,
                    kv.at[c, 4 * BACK + zz],
                    a5_snd.at[j],
                    p_sem.at[2 * BACK + j],
                    {"y": lax.rem(y + BACK, n_y)},
                )

            @pl.when(jnp.logical_not(mine))
            def _():
                send(unit, unit, x_snd.at[2 * d + j], x_sem.at[2 * d + j], {"x": x_mate})
                send(unit, unit, b_snd.at[4 * d + zz], c_sem.at[4 * d + zz], {"c": c_mate})

    def secondary(d):
        for j in range(2):
            zz = place(other_half, j)
            unit = kv.at[c, 4 * d + zz]

            @pl.when(jnp.logical_not((d == 0) & (zz == z)))
            def _():
                landed(unit, x_sem.at[2 * d + j])
                send(unit, unit, b_snd.at[4 * d + zz], c_sem.at[4 * d + zz], {"c": c_mate})

    def complete(d):
        for zz in range(4):

            @pl.when(jnp.logical_not((d == 0) & (zz == z)))
            def _():
                landed(kv.at[c_mate, 4 * d + zz], c_sem.at[4 * d + zz])

    score_scale = HEAD_DIM ** (-0.5)
    rows_per = 128

    def attend(d):
        def chunk(i, carry):
            first = pl.multiple_of(i * rows_per, rows_per)
            rows = pl.ds(first, rows_per)
            query = sq[rows, :]
            query_doc = dq[rows, :][:, :1]
            line_id = lax.broadcasted_iota(jnp.int32, (rows_per, toks), 0) + first
            query_pos = lax.shift_right_logical(line_id, 1) + z * toks
            key_id = lax.broadcasted_iota(jnp.int32, (rows_per, toks), 1)
            scores = []
            for zz in range(4):
                slot = 4 * d + zz
                tile = kv[0, slot, toks : toks + 16, :].astype(F32)
                key_doc = jnp.concatenate([tile[k : k + 1] for k in range(toks // 128)], axis=1)
                seen = (key_doc == query_doc) & (key_id + (zz - 4 * d) * toks <= query_pos)
                score = dot_nt(query, kv[0, slot, 0:toks, :])
                scores.append(jnp.where(seen, score, LOW))
            top = functools.reduce(jnp.maximum, scores)
            old_top = m_scr[rows, :][:, :1]
            new_top = jnp.maximum(old_top, jnp.max(top, axis=1, keepdims=True))
            shrink = jnp.exp((old_top - new_top) * score_scale)
            exps = [jnp.exp((score - new_top) * score_scale) for score in scores]
            added = jnp.sum(functools.reduce(jnp.add, exps), axis=1, keepdims=True)
            weighted = jnp.zeros((rows_per, HEAD_DIM), F32)
            for zz in range(4):
                weighted = weighted + dot_nn(exps[zz].astype(BF16), kv[1, 4 * d + zz, 0:toks, :])
            m_scr[rows, :] = jnp.broadcast_to(new_top, (rows_per, 128))
            l_scr[rows, :] = l_scr[rows, :] * shrink + added
            acc[rows, :] = acc[rows, :] * shrink + weighted
            return carry

        lax.fori_loop(0, 2 * toks // rows_per, chunk, 0)

    def row_prefixes():
        run_state[...] = jnp.zeros_like(run_state)
        run_decay[...] = jnp.zeros_like(run_decay)
        pdoc[...] = jnp.full_like(pdoc, -1.0)
        for d in range(1, BACK + 1):

            @pl.when(y >= d)
            def _(d=d):
                landed(t_in.at[d], t_sem.at[d])
                line = from_parts(t_in[d, 64:80, :])
                end = line[:, 2:3]
                if d == 1:
                    pdoc[...] = jnp.broadcast_to(end, pdoc.shape)
                for h in range(2):
                    rows = slice(32 * h, 32 * h + 32)
                    passed = run_decay[0:1, h : h + 1]
                    keep = jnp.where(end == pdoc[0:1, 0:1], jnp.exp(passed), 0.0)
                    run_state[rows, :] = run_state[rows, :] + t_in[d, rows, :].astype(F32) * keep
                run_decay[...] = run_decay[...] + line

        before = pdoc[0:1, 0:1]
        for h in range(2):
            rows = slice(32 * h, 32 * h + 32)
            entry = run_state[rows, :]
            p_out[0, rows, :] = entry.astype(BF16)
            for k in range(1, 4):
                prior = entry * weight_of(0, k - 1, h, before)
                for j in range(k):
                    part = s_in[j, rows, :].astype(F32)
                    if j < k - 1:
                        part = part * weight_of(j + 1, k - 1, h, ends[j])
                    prior = prior + part
                p_out[k, rows, :] = prior.astype(BF16)
        own_doc = before
        for k in range(1, 4):
            own_doc = jnp.where(z == k, ends[k - 1], own_doc)
        pdoc[...] = jnp.broadcast_to(own_doc, pdoc.shape)
        p_in[z] = p_out[z]
        for k in range(1, n_z):
            z2 = lax.rem(z + k, n_z)
            send(p_out.at[z2], p_in.at[z], p_snd.at[k - 1], st_sem.at[z], {"z": z2})

    def carry_over():
        for k in range(1, n_z):
            z2 = lax.rem(z + k, n_z)
            landed(p_in.at[z2], st_sem.at[z2])
        opened = (dcol[...][:, :1] == pdoc[0:1, 0:1]).astype(F32)
        squares = jnp.zeros((toks, 128), F32)
        for h in range(2):
            rows = slice(32 * h, 32 * h + 32)
            state = jnp.concatenate([p_in[q, rows, :] for q in range(4)], axis=0)
            query = wq[pl.ds(h, toks, stride=2), :].astype(BF16)
            factor = jnp.exp(ccol[...][:, h : h + 1]) * opened
            mixed = mix[h] + dot_nn(query, state) * factor
            mix[h] = mixed
            squares = squares + mixed * mixed
        sums = dot_nt(jnp.ones((8, 128), F32), squares, precision=lax.Precision.HIGHEST)
        ss_in[tp] = sums[0:1, :]

        def post(k, carry):
            send(ss_in.at[tp], ss_in.at[tp], ss_snd.at[k], ss_sem.at[tp], tp_place(k))
            return carry

        lax.fori_loop(1, n_tp, post, 0)

    def finish_lin():
        def arrive(k, carry):
            t2 = lax.rem(tp + k, n_tp)
            landed(ss_in.at[t2], ss_sem.at[t2])
            return carry

        lax.fori_loop(1, n_tp, arrive, 0)
        total = jnp.sum(ss_in[...], axis=0)
        inv = lax.rsqrt(total / (n_tp * 2 * HEAD_DIM) + 1e-06)
        inv_col = as_column(inv, toks)
        for h in range(2):
            gate = wg[pl.ds(h, toks, stride=2), :]
            wo[pl.ds(h, toks, stride=2), :] = (
                mix[h] * inv_col * gain[h : h + 1, :] * jax.nn.sigmoid(gate)
            )
        lin_out[...] = wo[...].astype(BF16)

    def order(it):
        return jnp.where(it == 4, 5, jnp.where(it == 5, 4, it))

    primary(0)

    def step(it, carry):
        d = order(it)
        after = order(it + 1)

        @pl.when(d <= y)
        def _():
            secondary(d)

        @pl.when((it < BACK) & (after <= y))
        def _():
            primary(after)

        @pl.when(d <= y)
        def _():
            complete(d)
            attend(d)

        @pl.when(it == 0)
        def _():
            row_prefixes()

        @pl.when(it == 1)
        def _():
            carry_over()

        return carry

    lax.fori_loop(0, BACK + 1, step, 0)
    soft_out[...] = (acc[...] / l_scr[...]).astype(BF16)
    finish_lin()

    for k in range(n_z - 1):
        left(s_out.at[0], s_snd.at[k])
        left(p_out.at[0], p_snd.at[k])

        @pl.when(owner)
        def _():
            left(kv.at[c, z], za_snd.at[k])

    for d in range(1, BACK + 1):

        @pl.when(y + d < n_y)
        def _(d=d):
            left(t_out, t_snd.at[d])

    def sent(k, carry):
        left(ss_in.at[tp], ss_snd.at[k])
        return carry

    lax.fori_loop(1, n_tp, sent, 0)

    def row_sent(d, carry):
        @pl.when(d <= y)
        def _():
            for j in range(2):
                mine = (d == 0) & (place(half, j) == z)

                @pl.when((y + 1 < n_y) & (d + 1 < BACK))
                def _():
                    left(kv.at[c, 0], a_snd.at[2 * d + j])

                @pl.when((y + BACK < n_y) & (d == 0))
                def _():
                    left(kv.at[c, 0], a5_snd.at[j])

                @pl.when(jnp.logical_not(mine))
                def _():
                    left(kv.at[c, 0], x_snd.at[2 * d + j])

            for zz in range(4):

                @pl.when(jnp.logical_not((d == 0) & (zz == z)))
                def _():
                    left(kv.at[c, 0], b_snd.at[4 * d + zz])

        return carry

    lax.fori_loop(0, BACK + 1, row_sent, 0)


def body(sizes, lin_query, lin_key, lin_value, lin_gate, log_decay, norm_gain, doc_ids,
         soft_query, soft_key, soft_value):
    toks = lin_query.shape[0]
    n_tp = sizes[2] * sizes[3] * sizes[4]
    flat = lambda a: a.reshape(-1, HEAD_DIM)
    dma = pltpu.SemaphoreType.DMA
    rows = BACK + 1
    unit = toks + 16
    in_vmem = pl.BlockSpec(memory_space=pltpu.VMEM)
    lin_out, soft_out = pl.pallas_call(
        functools.partial(kernel, sizes),
        out_shape=(
            jax.ShapeDtypeStruct((2 * toks, HEAD_DIM), BF16),
            jax.ShapeDtypeStruct((2 * toks, HEAD_DIM), BF16),
        ),
        in_specs=[in_vmem] * 10,
        out_specs=(in_vmem, in_vmem),
        scratch_shapes=[
            pltpu.VMEM((2, 4 * rows, unit, 128), BF16),
            pltpu.VMEM((2, KV_HEADS * toks, 128), F32),
            pltpu.VMEM((2 * toks, 128), F32),
            pltpu.VMEM((2 * toks, 128), F32),
            pltpu.VMEM((2 * toks, 128), F32),
            pltpu.VMEM((2 * toks, 128), F32),
            pltpu.VMEM((2 * toks, 128), F32),
            pltpu.VMEM((8, toks), F32),
            pltpu.VMEM((toks, 8), F32),
            pltpu.VMEM((toks, 128), F32),
            pltpu.VMEM((2 * toks, 128), F32),
            pltpu.VMEM((2, toks, 128), F32),
            pltpu.VMEM((4, 80, 128), BF16),
            pltpu.VMEM((4, 80, 128), BF16),
            pltpu.VMEM((80, 128), BF16),
            pltpu.VMEM((rows, 80, 128), BF16),
            pltpu.VMEM((4, 64, 128), BF16),
            pltpu.VMEM((4, 64, 128), BF16),
            pltpu.VMEM((64, 128), F32),
            pltpu.VMEM((1, 128), F32),
            pltpu.VMEM((1, 128), F32),
            pltpu.VMEM((n_tp, 1, toks), F32),
            pltpu.VMEM((2 * toks, 128), F32),
            pltpu.VMEM((2 * toks, 128), F32),
            pltpu.VMEM((2 * toks, 128), F32),
            dma((2 * rows,)),
            dma((2 * rows,)),
            dma((4 * rows,)),
            dma((4,)),
            dma((rows,)),
            dma((4,)),
            dma((n_tp,)),
            dma((3,)),
            dma((2 * rows,)),
            dma((2,)),
            dma((4 * rows,)),
            dma((2 * rows,)),
            dma((3,)),
            dma((rows,)),
            dma((3,)),
            dma((n_tp,)),
        ],
        compiler_params=pltpu.CompilerParams(
            collective_id=0, has_side_effects=True, vmem_limit_bytes=48 * 1024 * 1024
        ),
    )(
        flat(lin_query),
        flat(lin_key),
        flat(lin_value),
        flat(lin_gate),
        jnp.transpose(log_decay),
        norm_gain,
        doc_ids.reshape(1, toks),
        flat(soft_query),
        flat(soft_key),
        flat(soft_value),
    )
    return lin_out.reshape(toks, 2, HEAD_DIM), soft_out.reshape(toks, 2, HEAD_DIM)


def solution(mesh, sizes=(8, 4, 2, 8, 2)):
    split = Mesh(mesh.devices.reshape(sizes), ("y", "z", "w", "x", "c"))
    placed = (
        P(SEQ, TP, None),
        P(SEQ, TP, None),
        P(SEQ, TP, None),
        P(SEQ, TP, None),
        P(SEQ, TP),
        P(TP, None),
        P(SEQ),
        P(SEQ, TP, None),
        P(SEQ, None, None),
        P(SEQ, None, None),
    )
    return jax.shard_map(
        functools.partial(body, sizes),
        mesh=split,
        in_specs=placed,
        out_specs=(P(SEQ, TP, None), P(SEQ, TP, None)),
        check_vma=False,
    )
```

```python
import functools

import jax
import jax.numpy as jnp
from jax import lax
from jax.experimental import pallas as pl
from jax.experimental.pallas import tpu as pltpu
from jax.sharding import Mesh
from jax.sharding import PartitionSpec as P

HEADS = 64
HEAD_DIM = 128
KV_HEADS = 8
SEQ = ("y", "z")
TP = ("w", "x", "c")
MESH = pl.DeviceIdType.MESH
F32 = jnp.float32
BF16 = jnp.bfloat16
BACK = 5
LOW = -1e30


def dot_nt(a, b, **kw):
    return lax.dot_general(a, b, (((1,), (1,)), ((), ())), preferred_element_type=F32, **kw)


def dot_tn(a, b):
    return lax.dot_general(a, b, (((0,), (0,)), ((), ())), preferred_element_type=F32)


def dot_nn(a, b):
    return lax.dot_general(a, b, (((1,), (0,)), ((), ())), preferred_element_type=F32)


def as_column(row, toks):
    return jnp.concatenate(
        [
            jnp.transpose(jnp.broadcast_to(row[:, k : k + 128], (128, 128)))
            for k in range(0, toks, 128)
        ],
        axis=0,
    )


def three_parts(line):
    high = line.astype(BF16)
    rest = line - high.astype(F32)
    middle = rest.astype(BF16)
    low = (rest - middle.astype(F32)).astype(BF16)
    row = lax.broadcasted_iota(jnp.int32, (16, 128), 0)
    parts = [jnp.broadcast_to(p.astype(F32), (16, 128)) for p in (high, middle, low)]
    return jnp.where(
        row == 0, parts[0], jnp.where(row == 1, parts[1], jnp.where(row == 2, parts[2], 0.0))
    ).astype(BF16)


def from_parts(tile):
    wide = tile.astype(F32)
    return wide[0:1] + wide[1:2] + wide[2:3]


def kernel(
    sizes,
    lq_in,
    lk_in,
    lv_in,
    lg_in,
    ld_in,
    gain_in,
    docs_in,
    sq_in,
    sk_in,
    sv_in,
    lin_out,
    soft_out,
    lq,
    lk,
    lv,
    lg,
    ld,
    gain,
    docs,
    sq,
    sk,
    sv,
    in_sem,
    kv,
    wide8,
    wq,
    wk,
    wv,
    wg,
    wo,
    dec,
    ccol,
    dcol,
    dq,
    mix,
    s_out,
    s_in,
    t_out,
    t_in,
    p_out,
    p_in,
    run_state,
    run_decay,
    pdoc,
    ss_in,
    m_scr,
    l_scr,
    acc,
    p_sem,
    x_sem,
    c_sem,
    s_sem,
    t_sem,
    st_sem,
    ss_sem,
    ready,
    za_snd,
    a_snd,
    a5_snd,
    b_snd,
    x_snd,
    s_snd,
    t_snd,
    p_snd,
    ss_snd,
):
    n_y, n_z, n_w, n_x, n_c = sizes
    n_tp = n_w * n_x * n_c
    toks = docs.shape[1]
    y, z, w = (lax.axis_index("y"), lax.axis_index("z"), lax.axis_index("w"))
    x, c = (lax.axis_index("x"), lax.axis_index("c"))
    tp = (w * n_x + x) * n_c + c
    half = lax.rem(x, 2)
    other_half = 1 - half
    x_mate = x + 1 - 2 * half
    c_mate = 1 - c
    head = (tp * 2) // (HEADS // KV_HEADS)

    def tp_place(k):
        t2 = lax.rem(tp + k, n_tp)
        return {"w": t2 // (n_x * n_c), "x": lax.rem(t2 // n_c, n_x), "c": lax.rem(t2, n_c)}

    def turn(w_, x_, c_):
        apart = jnp.minimum(x_, n_x - x_)
        step = 2 * apart - jnp.where((x_ >= 1) & (2 * x_ <= n_x), 1, 0)
        return (w_ * n_x + step) * n_c + c_

    own_turn = turn(w, x, c)
    barrier = pltpu.get_barrier_semaphore()

    def greet_tp(k, carry):
        other = tp_place(k)
        near = ((other["x"] == x) | ((other["x"] == x_mate) & (other["c"] == c))) & (other["w"] == w)

        @pl.when(near | (turn(other["w"], other["x"], other["c"]) > own_turn))
        def _():
            pl.semaphore_signal(barrier, inc=1, device_id=other, device_id_type=MESH)

        return carry

    def tell_tp(k, carry):
        other = tp_place(k)

        @pl.when(turn(other["w"], other["x"], other["c"]) < own_turn)
        def _():
            pl.semaphore_signal(ready, inc=1, device_id=other, device_id_type=MESH)

        return carry

    def greet_y(k, carry):
        pl.semaphore_signal(
            barrier, inc=1, device_id={"y": lax.rem(y + k, n_y)}, device_id_type=MESH
        )
        return carry

    loads = [
        pltpu.make_async_copy(source, target, in_sem.at[k])
        for k, (source, target) in enumerate(
            (
                (sk_in, sk),
                (sv_in, sv),
                (docs_in, docs),
                (ld_in, ld),
                (lk_in, lk),
                (lv_in, lv),
                (lq_in, lq),
                (lg_in, lg),
                (sq_in, sq),
                (gain_in, gain),
            )
        )
    ]
    for load in loads:
        load.start()
    for k in range(1, n_z):
        pl.semaphore_signal(
            barrier, inc=1, device_id={"z": lax.rem(z + k, n_z)}, device_id_type=MESH
        )
    lax.fori_loop(1, n_y, greet_y, 0)
    lax.fori_loop(1, n_tp, greet_tp, 0)

    def send(src, dst, send_sem, recv_sem, device):
        pltpu.make_async_remote_copy(
            src_ref=src,
            dst_ref=dst,
            send_sem=send_sem,
            recv_sem=recv_sem,
            device_id=device,
            device_id_type=MESH,
        ).start()

    def landed(ref, sem):
        pltpu.make_async_remote_copy(
            src_ref=ref,
            dst_ref=ref,
            send_sem=a5_snd.at[0],
            recv_sem=sem,
            device_id={"c": c_mate},
            device_id_type=MESH,
        ).wait_recv()

    def left(ref, sem):
        pltpu.make_async_remote_copy(
            src_ref=ref,
            dst_ref=ref,
            send_sem=sem,
            recv_sem=p_sem.at[0],
            device_id={"c": c_mate},
            device_id_type=MESH,
        ).wait_send()

    for load in loads[:3]:
        load.wait()
    doc_row = docs[...].astype(F32)
    pack_row = lax.broadcasted_iota(jnp.int32, (16, 128), 0)
    doc_tile = jnp.zeros((16, 128), F32)
    for k in range(toks // 128):
        piece = jnp.broadcast_to(doc_row[:, 128 * k : 128 * (k + 1)], (16, 128))
        doc_tile = jnp.where(pack_row == k, piece, doc_tile)
    doc_tile = doc_tile.astype(BF16)
    for kind, source in ((0, sk), (1, sv)):
        wide8[kind] = source[...].astype(F32)
        kv[kind, z, 0:toks, :] = wide8[kind, pl.ds(head, toks, stride=KV_HEADS), :].astype(BF16)
        kv[kind, z, toks : toks + 16, :] = doc_tile

    doc_col = as_column(doc_row, toks)
    dcol[...] = doc_col
    for h in range(2):
        dq[pl.ds(h, toks, stride=2), :] = doc_col
    for load in loads[3:]:
        load.wait()
    for source, target in ((lq, wq), (lk, wk), (lv, wv), (lg, wg)):
        target[...] = source[...].astype(F32)

    dec[...] = jnp.zeros_like(dec)
    dec[0:2, :] = ld[...]
    t_id = lax.broadcasted_iota(jnp.int32, (toks, toks), 0)
    s_id = lax.broadcasted_iota(jnp.int32, (toks, toks), 1)
    upto = (s_id <= t_id).astype(F32)
    cum_col = dot_nt(upto, dec[...], precision=lax.Precision.HIGHEST)
    cum_row = dot_nt(dec[...], upto, precision=lax.Precision.HIGHEST)
    ccol[...] = cum_col
    last_doc = doc_row[:, toks - 1 : toks]
    tail = (doc_col[:, :1] == last_doc).astype(F32)
    queries = [wq[pl.ds(h, toks, stride=2), :].astype(BF16) for h in range(2)]
    keys = [wk[pl.ds(h, toks, stride=2), :] for h in range(2)]
    values = [wv[pl.ds(h, toks, stride=2), :].astype(BF16) for h in range(2)]
    decay_line = jnp.zeros((1, 128), F32)
    lane = lax.broadcasted_iota(jnp.int32, (1, 128), 1)
    for h in range(2):
        end = cum_col[toks - 1 : toks, h : h + 1]
        scale = jnp.exp(end - cum_col[:, h : h + 1]) * tail
        state = dot_tn((keys[h] * scale).astype(BF16), values[h]).astype(BF16)
        for q in range(4):
            s_out[q, 32 * h : 32 * h + 32, :] = state[32 * q : 32 * q + 32, :]
        decay_line = jnp.where(lane == h, end, decay_line)
    decay_line = jnp.where(lane == 2, last_doc, decay_line)
    scalars = three_parts(decay_line)
    for q in range(4):
        s_out[q, 64:80, :] = scalars
    s_in[z] = s_out[z]
    for zz in range(4):
        in_half = ((zz == 0) or (zz == 3)) == (half == 0)
        for kind in range(2):

            @pl.when((zz > z) & jnp.logical_not(in_half & (c == kind)))
            def _(zz=zz, kind=kind):
                kv[kind, zz] = jnp.full(kv.shape[2:], -1.0, BF16)

            @pl.when((zz < z) & (y >= BACK))
            def _(zz=zz, kind=kind):
                kv[kind, 4 * BACK + zz] = jnp.full(kv.shape[2:], -1.0, BF16)

    early_mates = c + jnp.where(turn(w, x_mate, c) < own_turn, 1, 0)
    pl.semaphore_wait(barrier, (n_z - 1) + (n_y - 1) + 2 + own_turn - early_mates)

    for k in range(1, n_z):
        z2 = lax.rem(z + k, n_z)
        send(s_out.at[z2], s_in.at[z], s_snd.at[k - 1], s_sem.at[z], {"z": z2})
    owner = ((z == 0) | (z == 3)) == (half == 0)

    @pl.when(owner)
    def _():
        for k in range(1, n_z):
            z2 = lax.rem(z + jnp.where(z < 2, n_z - k, k), n_z)
            send(kv.at[c, z], kv.at[c, z], za_snd.at[k - 1], p_sem.at[z // 2], {"z": z2})

    lax.fori_loop(1, n_tp, tell_tp, 0)
    visible = (s_id <= t_id) & (doc_row == doc_col[:, :1])
    for h in range(2):
        gap = cum_col[:, h : h + 1] - cum_row[h : h + 1, :]
        factor = jnp.where(visible, jnp.exp(jnp.where(visible, gap, 0.0)), 0.0)
        weights = (dot_nt(queries[h], keys[h].astype(BF16)) * factor).astype(BF16)
        mix[h] = dot_nn(weights, values[h])
    m_scr[...] = jnp.full_like(m_scr, LOW)
    l_scr[...] = jnp.zeros_like(l_scr)
    acc[...] = jnp.zeros_like(acc)

    for k in range(1, n_z):
        z2 = lax.rem(z + k, n_z)
        landed(s_in.at[z2], s_sem.at[z2])
    lines = [from_parts(s_in[k, 64:80, :]) for k in range(4)]
    ends = [line[:, 2:3] for line in lines]

    def weight_of(first, last, h, doc):
        total = jnp.zeros((1, 1), F32)
        for k in range(first, last + 1):
            total = total + lines[k][:, h : h + 1]
        return jnp.where(doc == ends[last], jnp.exp(total), 0.0)

    total_line = lines[0] + lines[1] + lines[2] + lines[3]
    for h in range(2):
        rows = slice(32 * h, 32 * h + 32)
        total = s_in[3, rows, :].astype(F32)
        for k in range(3):
            total = total + s_in[k, rows, :].astype(F32) * weight_of(k + 1, 3, h, ends[k])
        t_out[rows, :] = total.astype(BF16)
    t_out[64:80, :] = three_parts(jnp.where(lane == 2, ends[3], total_line))
    for d in range(1, BACK + 1):

        @pl.when(y + d < n_y)
        def _(d=d):
            send(t_out, t_in.at[d], t_snd.at[d], t_sem.at[d], {"y": y + d})

    def place(which, j):
        return which + j * (3 - 2 * which)

    def seen_here(d, zz):
        return jnp.logical_not(((d == 0) & (zz >= z)) | ((d == BACK) & (zz < z)))

    def primary(d):
        for j in range(2):
            zz = place(half, j)
            unit = kv.at[c, 4 * d + zz]

            @pl.when(jnp.logical_not(((d == 0) & (zz == z)) | ((d == BACK) & (zz < z))))
            def _():
                landed(unit, p_sem.at[2 * d + j])

            @pl.when((y + 1 < n_y) & (d + 1 < BACK))
            def _():
                send(
                    unit,
                    kv.at[c, 4 * d + 4 + zz],
                    a_snd.at[2 * d + j],
                    p_sem.at[2 * d + 2 + j],
                    {"y": lax.rem(y + 1, n_y)},
                )

            @pl.when((y + BACK < n_y) & (d == 0) & (zz >= z))
            def _():
                send(
                    unit,
                    kv.at[c, 4 * BACK + zz],
                    a5_snd.at[j],
                    p_sem.at[2 * BACK + j],
                    {"y": lax.rem(y + BACK, n_y)},
                )

            @pl.when(seen_here(d, zz))
            def _():
                send(unit, unit, x_snd.at[2 * d + j], x_sem.at[2 * d + j], {"x": x_mate})
                send(unit, unit, b_snd.at[4 * d + zz], c_sem.at[4 * d + zz], {"c": c_mate})

    def secondary(d):
        for j in range(2):
            zz = place(other_half, j)
            unit = kv.at[c, 4 * d + zz]

            @pl.when(seen_here(d, zz))
            def _():
                landed(unit, x_sem.at[2 * d + j])
                send(unit, unit, b_snd.at[4 * d + zz], c_sem.at[4 * d + zz], {"c": c_mate})

    def complete(d):
        for zz in range(4):

            @pl.when(seen_here(d, zz))
            def _():
                landed(kv.at[c_mate, 4 * d + zz], c_sem.at[4 * d + zz])

    score_scale = HEAD_DIM ** (-0.5)
    rows_per = 128

    def attend(d):
        def chunk(i, carry):
            first = pl.multiple_of(i * rows_per, rows_per)
            rows = pl.ds(first, rows_per)
            query = sq[rows, :]
            query_doc = dq[rows, :][:, :1]
            line_id = lax.broadcasted_iota(jnp.int32, (rows_per, toks), 0) + first
            query_pos = lax.shift_right_logical(line_id, 1) + z * toks
            key_id = lax.broadcasted_iota(jnp.int32, (rows_per, toks), 1)
            scores = []
            for zz in range(4):
                slot = 4 * d + zz
                tile = kv[0, slot, toks : toks + 16, :].astype(F32)
                key_doc = jnp.concatenate([tile[k : k + 1] for k in range(toks // 128)], axis=1)
                seen = (key_doc == query_doc) & (key_id + (zz - 4 * d) * toks <= query_pos)
                score = dot_nt(query, kv[0, slot, 0:toks, :])
                scores.append(jnp.where(seen, score, LOW))
            top = functools.reduce(jnp.maximum, scores)
            old_top = m_scr[rows, :][:, :1]
            new_top = jnp.maximum(old_top, jnp.max(top, axis=1, keepdims=True))
            shrink = jnp.exp((old_top - new_top) * score_scale)
            exps = [jnp.exp((score - new_top) * score_scale) for score in scores]
            added = jnp.sum(functools.reduce(jnp.add, exps), axis=1, keepdims=True)
            weighted = jnp.zeros((rows_per, HEAD_DIM), F32)
            for zz in range(4):
                weighted = weighted + dot_nn(exps[zz].astype(BF16), kv[1, 4 * d + zz, 0:toks, :])
            m_scr[rows, :] = jnp.broadcast_to(new_top, (rows_per, 128))
            l_scr[rows, :] = l_scr[rows, :] * shrink + added
            acc[rows, :] = acc[rows, :] * shrink + weighted
            return carry

        lax.fori_loop(0, 2 * toks // rows_per, chunk, 0)

    def row_prefixes():
        run_state[...] = jnp.zeros_like(run_state)
        run_decay[...] = jnp.zeros_like(run_decay)
        pdoc[...] = jnp.full_like(pdoc, -1.0)
        for d in range(1, BACK + 1):

            @pl.when(y >= d)
            def _(d=d):
                landed(t_in.at[d], t_sem.at[d])
                line = from_parts(t_in[d, 64:80, :])
                end = line[:, 2:3]
                if d == 1:
                    pdoc[...] = jnp.broadcast_to(end, pdoc.shape)
                for h in range(2):
                    rows = slice(32 * h, 32 * h + 32)
                    passed = run_decay[0:1, h : h + 1]
                    keep = jnp.where(end == pdoc[0:1, 0:1], jnp.exp(passed), 0.0)
                    run_state[rows, :] = run_state[rows, :] + t_in[d, rows, :].astype(F32) * keep
                run_decay[...] = run_decay[...] + line

        before = pdoc[0:1, 0:1]
        for h in range(2):
            rows = slice(32 * h, 32 * h + 32)
            entry = run_state[rows, :]
            p_out[0, rows, :] = entry.astype(BF16)
            for k in range(1, 4):
                prior = entry * weight_of(0, k - 1, h, before)
                for j in range(k):
                    part = s_in[j, rows, :].astype(F32)
                    if j < k - 1:
                        part = part * weight_of(j + 1, k - 1, h, ends[j])
                    prior = prior + part
                p_out[k, rows, :] = prior.astype(BF16)
        own_doc = before
        for k in range(1, 4):
            own_doc = jnp.where(z == k, ends[k - 1], own_doc)
        pdoc[...] = jnp.broadcast_to(own_doc, pdoc.shape)
        p_in[z] = p_out[z]
        for k in range(1, n_z):
            z2 = lax.rem(z + k, n_z)
            send(p_out.at[z2], p_in.at[z], p_snd.at[k - 1], st_sem.at[z], {"z": z2})

    def carry_over():
        for k in range(1, n_z):
            z2 = lax.rem(z + k, n_z)
            landed(p_in.at[z2], st_sem.at[z2])
        opened = (dcol[...][:, :1] == pdoc[0:1, 0:1]).astype(F32)
        squares = jnp.zeros((toks, 128), F32)
        for h in range(2):
            rows = slice(32 * h, 32 * h + 32)
            state = jnp.concatenate([p_in[q, rows, :] for q in range(4)], axis=0)
            query = wq[pl.ds(h, toks, stride=2), :].astype(BF16)
            factor = jnp.exp(ccol[...][:, h : h + 1]) * opened
            mixed = mix[h] + dot_nn(query, state) * factor
            mix[h] = mixed
            squares = squares + mixed * mixed
        sums = dot_nt(jnp.ones((8, 128), F32), squares, precision=lax.Precision.HIGHEST)
        ss_in[tp] = sums[0:1, :]

    def post_squares():
        @pl.when(own_turn < n_tp - 1)
        def _():
            pl.semaphore_wait(ready, n_tp - 1 - own_turn)

        def post(k, carry):
            send(ss_in.at[tp], ss_in.at[tp], ss_snd.at[k], ss_sem.at[tp], tp_place(k))
            return carry

        lax.fori_loop(1, n_tp, post, 0)

    def finish_lin():
        def arrive(k, carry):
            t2 = lax.rem(tp + k, n_tp)
            landed(ss_in.at[t2], ss_sem.at[t2])
            return carry

        lax.fori_loop(1, n_tp, arrive, 0)
        total = jnp.sum(ss_in[...], axis=0)
        inv = lax.rsqrt(total / (n_tp * 2 * HEAD_DIM) + 1e-06)
        inv_col = as_column(inv, toks)
        for h in range(2):
            gate = wg[pl.ds(h, toks, stride=2), :]
            wo[pl.ds(h, toks, stride=2), :] = (
                mix[h] * inv_col * gain[h : h + 1, :] * jax.nn.sigmoid(gate)
            )
        lin_out[...] = wo[...].astype(BF16)

    def order(it):
        return jnp.where(it == 4, 5, jnp.where(it == 5, 4, it))

    primary(0)

    post_at = jnp.where(w == 0, 4, 1)

    def step(it, carry):
        d = order(it)
        after = order(it + 1)

        @pl.when((it < BACK) & (after <= y))
        def _():
            primary(after)

        @pl.when(it == 0)
        def _():
            row_prefixes()

        @pl.when(it == 1)
        def _():
            carry_over()

        @pl.when(it == post_at)
        def _():
            post_squares()

        @pl.when(d <= y)
        def _():
            secondary(d)
            complete(d)
            attend(d)

        return carry

    lax.fori_loop(0, BACK + 1, step, 0)
    soft_out[...] = (acc[...] / l_scr[...]).astype(BF16)
    finish_lin()

    for k in range(n_z - 1):
        left(s_out.at[0], s_snd.at[k])
        left(p_out.at[0], p_snd.at[k])

        @pl.when(owner)
        def _():
            left(kv.at[c, z], za_snd.at[k])

    for d in range(1, BACK + 1):

        @pl.when(y + d < n_y)
        def _(d=d):
            left(t_out, t_snd.at[d])

    def sent(k, carry):
        left(ss_in.at[tp], ss_snd.at[k])
        return carry

    lax.fori_loop(1, n_tp, sent, 0)

    def row_sent(d, carry):
        @pl.when(d <= y)
        def _():
            for j in range(2):
                zz = place(half, j)

                @pl.when((y + 1 < n_y) & (d + 1 < BACK))
                def _():
                    left(kv.at[c, 0], a_snd.at[2 * d + j])

                @pl.when((y + BACK < n_y) & (d == 0) & (zz >= z))
                def _():
                    left(kv.at[c, 0], a5_snd.at[j])

                @pl.when(seen_here(d, zz))
                def _():
                    left(kv.at[c, 0], x_snd.at[2 * d + j])

            for zz in range(4):

                @pl.when(seen_here(d, zz))
                def _():
                    left(kv.at[c, 0], b_snd.at[4 * d + zz])

        return carry

    lax.fori_loop(0, BACK + 1, row_sent, 0)


def body(sizes, lin_query, lin_key, lin_value, lin_gate, log_decay, norm_gain, doc_ids,
         soft_query, soft_key, soft_value):
    toks = lin_query.shape[0]
    n_tp = sizes[2] * sizes[3] * sizes[4]
    flat = lambda a: a.reshape(-1, HEAD_DIM)
    dma = pltpu.SemaphoreType.DMA
    rows = BACK + 1
    unit = toks + 16
    in_vmem = pl.BlockSpec(memory_space=pltpu.VMEM)
    in_place = pl.BlockSpec(memory_space=pl.ANY)
    lin_out, soft_out = pl.pallas_call(
        functools.partial(kernel, sizes),
        out_shape=(
            jax.ShapeDtypeStruct((2 * toks, HEAD_DIM), BF16),
            jax.ShapeDtypeStruct((2 * toks, HEAD_DIM), BF16),
        ),
        in_specs=[in_place] * 10,
        out_specs=(in_vmem, in_vmem),
        scratch_shapes=[
            pltpu.VMEM((2 * toks, 128), BF16),
            pltpu.VMEM((2 * toks, 128), BF16),
            pltpu.VMEM((2 * toks, 128), BF16),
            pltpu.VMEM((2 * toks, 128), BF16),
            pltpu.VMEM((2, toks), F32),
            pltpu.VMEM((2, 128), F32),
            pltpu.VMEM((1, toks), jnp.int32),
            pltpu.VMEM((2 * toks, 128), BF16),
            pltpu.VMEM((KV_HEADS * toks, 128), BF16),
            pltpu.VMEM((KV_HEADS * toks, 128), BF16),
            dma((10,)),
            pltpu.VMEM((2, 4 * rows, unit, 128), BF16),
            pltpu.VMEM((2, KV_HEADS * toks, 128), F32),
            pltpu.VMEM((2 * toks, 128), F32),
            pltpu.VMEM((2 * toks, 128), F32),
            pltpu.VMEM((2 * toks, 128), F32),
            pltpu.VMEM((2 * toks, 128), F32),
            pltpu.VMEM((2 * toks, 128), F32),
            pltpu.VMEM((8, toks), F32),
            pltpu.VMEM((toks, 8), F32),
            pltpu.VMEM((toks, 128), F32),
            pltpu.VMEM((2 * toks, 128), F32),
            pltpu.VMEM((2, toks, 128), F32),
            pltpu.VMEM((4, 80, 128), BF16),
            pltpu.VMEM((4, 80, 128), BF16),
            pltpu.VMEM((80, 128), BF16),
            pltpu.VMEM((rows, 80, 128), BF16),
            pltpu.VMEM((4, 64, 128), BF16),
            pltpu.VMEM((4, 64, 128), BF16),
            pltpu.VMEM((64, 128), F32),
            pltpu.VMEM((1, 128), F32),
            pltpu.VMEM((1, 128), F32),
            pltpu.VMEM((n_tp, 1, toks), F32),
            pltpu.VMEM((2 * toks, 128), F32),
            pltpu.VMEM((2 * toks, 128), F32),
            pltpu.VMEM((2 * toks, 128), F32),
            dma((2 * rows,)),
            dma((2 * rows,)),
            dma((4 * rows,)),
            dma((4,)),
            dma((rows,)),
            dma((4,)),
            dma((n_tp,)),
            pltpu.SemaphoreType.REGULAR,
            dma((3,)),
            dma((2 * rows,)),
            dma((2,)),
            dma((4 * rows,)),
            dma((2 * rows,)),
            dma((3,)),
            dma((rows,)),
            dma((3,)),
            dma((n_tp,)),
        ],
        compiler_params=pltpu.CompilerParams(
            collective_id=0, has_side_effects=True, vmem_limit_bytes=56 * 1024 * 1024
        ),
    )(
        flat(lin_query),
        flat(lin_key),
        flat(lin_value),
        flat(lin_gate),
        jnp.transpose(log_decay),
        norm_gain,
        doc_ids.reshape(1, toks),
        flat(soft_query),
        flat(soft_key),
        flat(soft_value),
    )
    return lin_out.reshape(toks, 2, HEAD_DIM), soft_out.reshape(toks, 2, HEAD_DIM)


def solution(mesh, sizes=(8, 4, 2, 8, 2)):
    split = Mesh(mesh.devices.reshape(sizes), ("y", "z", "w", "x", "c"))
    placed = (
        P(SEQ, TP, None),
        P(SEQ, TP, None),
        P(SEQ, TP, None),
        P(SEQ, TP, None),
        P(SEQ, TP),
        P(TP, None),
        P(SEQ),
        P(SEQ, TP, None),
        P(SEQ, None, None),
        P(SEQ, None, None),
    )
    return jax.shard_map(
        functools.partial(body, sizes),
        mesh=split,
        in_specs=placed,
        out_specs=(P(SEQ, TP, None), P(SEQ, TP, None)),
        check_vma=False,
    )
```

```python
import functools
import math

import jax
import jax.numpy as jnp
from jax import lax
from jax.experimental import pallas as pl
from jax.experimental.pallas import tpu as pltpu
from jax.sharding import Mesh
from jax.sharding import PartitionSpec as P

HEADS = 64
HEAD_DIM = 128
KV_HEADS = 8
SEQ = ("y", "z")
TP = ("w", "x", "c")
MESH = pl.DeviceIdType.MESH
F32 = jnp.float32
BF16 = jnp.bfloat16
BACK = 5
LOW = -1e30


def dot_nt(a, b, **kw):
    return lax.dot_general(a, b, (((1,), (1,)), ((), ())), preferred_element_type=F32, **kw)


def dot_tn(a, b):
    return lax.dot_general(a, b, (((0,), (0,)), ((), ())), preferred_element_type=F32)


def dot_nn(a, b):
    return lax.dot_general(a, b, (((1,), (0,)), ((), ())), preferred_element_type=F32)


def as_column(row, toks):
    return jnp.concatenate(
        [
            jnp.transpose(jnp.broadcast_to(row[:, k : k + 128], (128, 128)))
            for k in range(0, toks, 128)
        ],
        axis=0,
    )


def three_parts(line):
    high = line.astype(BF16)
    rest = line - high.astype(F32)
    middle = rest.astype(BF16)
    low = (rest - middle.astype(F32)).astype(BF16)
    row = lax.broadcasted_iota(jnp.int32, (16, 128), 0)
    parts = [jnp.broadcast_to(p.astype(F32), (16, 128)) for p in (high, middle, low)]
    return jnp.where(
        row == 0, parts[0], jnp.where(row == 1, parts[1], jnp.where(row == 2, parts[2], 0.0))
    ).astype(BF16)


def from_parts(tile):
    wide = tile.astype(F32)
    return wide[0:1] + wide[1:2] + wide[2:3]


def kernel(
    sizes,
    lq_in,
    lk_in,
    lv_in,
    lg_in,
    ld_in,
    gain_in,
    docs_in,
    sq_in,
    sk_in,
    sv_in,
    lin_out,
    soft_out,
    lq,
    lk,
    lv,
    lg,
    ld,
    gain,
    docs,
    sq,
    sk,
    sv,
    in_sem,
    kv,
    wide8,
    wq,
    wk,
    wv,
    wg,
    wo,
    dec,
    ccol,
    dcol,
    dq,
    mix,
    s_out,
    s_in,
    t_out,
    t_in,
    p_out,
    p_in,
    run_state,
    run_decay,
    pdoc,
    ss_in,
    m_scr,
    l_scr,
    acc,
    p_sem,
    x_sem,
    c_sem,
    s_sem,
    t_sem,
    st_sem,
    ss_sem,
    ready,
    za_snd,
    a_snd,
    a5_snd,
    b_snd,
    x_snd,
    s_snd,
    t_snd,
    p_snd,
    ss_snd,
):
    n_y, n_z, n_w, n_x, n_c = sizes
    n_tp = n_w * n_x * n_c
    toks = docs.shape[1]
    y, z, w = (lax.axis_index("y"), lax.axis_index("z"), lax.axis_index("w"))
    x, c = (lax.axis_index("x"), lax.axis_index("c"))
    tp = (w * n_x + x) * n_c + c
    half = lax.rem(x, 2)
    other_half = 1 - half
    x_mate = x + 1 - 2 * half
    c_mate = 1 - c
    head = (tp * 2) // (HEADS // KV_HEADS)

    def tp_place(k):
        t2 = lax.rem(tp + k, n_tp)
        return {"w": t2 // (n_x * n_c), "x": lax.rem(t2 // n_c, n_x), "c": lax.rem(t2, n_c)}

    def turn(w_, x_, c_):
        apart = jnp.minimum(x_, n_x - x_)
        step = 2 * apart - jnp.where((x_ >= 1) & (2 * x_ <= n_x), 1, 0)
        return (w_ * n_x + step) * n_c + c_

    own_turn = turn(w, x, c)
    barrier = pltpu.get_barrier_semaphore()

    def greet_tp(k, carry):
        other = tp_place(k)
        near = ((other["x"] == x) | ((other["x"] == x_mate) & (other["c"] == c))) & (other["w"] == w)

        @pl.when(near | (turn(other["w"], other["x"], other["c"]) > own_turn))
        def _():
            pl.semaphore_signal(barrier, inc=1, device_id=other, device_id_type=MESH)

        return carry

    def tell_tp(k, carry):
        other = tp_place(k)

        @pl.when(turn(other["w"], other["x"], other["c"]) < own_turn)
        def _():
            pl.semaphore_signal(ready, inc=1, device_id=other, device_id_type=MESH)

        return carry

    def greet_y(k, carry):
        pl.semaphore_signal(
            barrier, inc=1, device_id={"y": lax.rem(y + k, n_y)}, device_id_type=MESH
        )
        return carry

    loads = [
        pltpu.make_async_copy(source, target, in_sem.at[k])
        for k, (source, target) in enumerate(
            (
                (sk_in, sk),
                (sv_in, sv),
                (docs_in, docs),
                (ld_in, ld),
                (lk_in, lk),
                (lv_in, lv),
                (lq_in, lq),
                (lg_in, lg),
                (sq_in, sq),
                (gain_in, gain),
            )
        )
    ]
    for load in loads:
        load.start()
    for k in range(1, n_z):
        pl.semaphore_signal(
            barrier, inc=1, device_id={"z": lax.rem(z + k, n_z)}, device_id_type=MESH
        )
    lax.fori_loop(1, n_y, greet_y, 0)
    lax.fori_loop(1, n_tp, greet_tp, 0)

    def send(src, dst, send_sem, recv_sem, device):
        pltpu.make_async_remote_copy(
            src_ref=src,
            dst_ref=dst,
            send_sem=send_sem,
            recv_sem=recv_sem,
            device_id=device,
            device_id_type=MESH,
        ).start()

    def landed(ref, sem):
        pltpu.make_async_remote_copy(
            src_ref=ref,
            dst_ref=ref,
            send_sem=a5_snd.at[0],
            recv_sem=sem,
            device_id={"c": c_mate},
            device_id_type=MESH,
        ).wait_recv()

    def left(ref, sem):
        pltpu.make_async_remote_copy(
            src_ref=ref,
            dst_ref=ref,
            send_sem=sem,
            recv_sem=p_sem.at[0],
            device_id={"c": c_mate},
            device_id_type=MESH,
        ).wait_send()

    for load in loads[:3]:
        load.wait()
    doc_row = docs[...].astype(F32)
    pack_row = lax.broadcasted_iota(jnp.int32, (16, 128), 0)
    doc_tile = jnp.zeros((16, 128), F32)
    for k in range(toks // 128):
        piece = jnp.broadcast_to(doc_row[:, 128 * k : 128 * (k + 1)], (16, 128))
        doc_tile = jnp.where(pack_row == k, piece, doc_tile)
    doc_tile = doc_tile.astype(BF16)
    for kind, source in ((0, sk), (1, sv)):
        wide8[kind] = source[...].astype(F32)
        kv[kind, z, 0:toks, :] = wide8[kind, pl.ds(head, toks, stride=KV_HEADS), :].astype(BF16)
        kv[kind, z, toks : toks + 16, :] = doc_tile

    doc_col = as_column(doc_row, toks)
    for load in loads[3:6]:
        load.wait()
    for source, target in ((lk, wk), (lv, wv)):
        target[...] = source[...].astype(F32)

    dec[...] = jnp.zeros_like(dec)
    dec[0:2, :] = ld[...]
    t_id = lax.broadcasted_iota(jnp.int32, (toks, toks), 0)
    s_id = lax.broadcasted_iota(jnp.int32, (toks, toks), 1)
    upto = (s_id <= t_id).astype(F32)
    cum_col = dot_nt(upto, dec[...], precision=lax.Precision.HIGHEST)
    cum_row = dot_nt(dec[...], upto, precision=lax.Precision.HIGHEST)
    ccol[...] = cum_col
    last_doc = doc_row[:, toks - 1 : toks]
    tail = (doc_col[:, :1] == last_doc).astype(F32)
    keys = [wk[pl.ds(h, toks, stride=2), :] for h in range(2)]
    values = [wv[pl.ds(h, toks, stride=2), :].astype(BF16) for h in range(2)]
    decay_line = jnp.zeros((1, 128), F32)
    lane = lax.broadcasted_iota(jnp.int32, (1, 128), 1)
    for h in range(2):
        end = cum_col[toks - 1 : toks, h : h + 1]
        scale = jnp.exp(end - cum_col[:, h : h + 1]) * tail
        state = dot_tn((keys[h] * scale).astype(BF16), values[h]).astype(BF16)
        for q in range(4):
            s_out[q, 32 * h : 32 * h + 32, :] = state[32 * q : 32 * q + 32, :]
        decay_line = jnp.where(lane == h, end, decay_line)
    decay_line = jnp.where(lane == 2, last_doc, decay_line)
    scalars = three_parts(decay_line)
    for q in range(4):
        s_out[q, 64:80, :] = scalars
    s_in[z] = s_out[z]
    for zz in range(4):
        in_half = ((zz == 0) or (zz == 3)) == (half == 0)
        for kind in range(2):

            @pl.when((zz > z) & jnp.logical_not(in_half & (c == kind)))
            def _(zz=zz, kind=kind):
                kv[kind, zz] = jnp.full(kv.shape[2:], -1.0, BF16)

            @pl.when((zz < z) & (y >= BACK))
            def _(zz=zz, kind=kind):
                kv[kind, 4 * BACK + zz] = jnp.full(kv.shape[2:], -1.0, BF16)

    early_mates = c + jnp.where(turn(w, x_mate, c) < own_turn, 1, 0)
    pl.semaphore_wait(barrier, (n_z - 1) + (n_y - 1) + 2 + own_turn - early_mates)

    for k in range(1, n_z):
        z2 = lax.rem(z + k, n_z)
        send(s_out.at[z2], s_in.at[z], s_snd.at[k - 1], s_sem.at[z], {"z": z2})
    owner = ((z == 0) | (z == 3)) == (half == 0)

    @pl.when(owner)
    def _():
        for k in range(1, n_z):
            z2 = lax.rem(z + jnp.where(z < 2, n_z - k, k), n_z)
            send(kv.at[c, z], kv.at[c, z], za_snd.at[k - 1], p_sem.at[z // 2], {"z": z2})

    lax.fori_loop(1, n_tp, tell_tp, 0)
    dcol[...] = doc_col
    for h in range(2):
        dq[pl.ds(h, toks, stride=2), :] = doc_col
    for load in loads[6:]:
        load.wait()
    for source, target in ((lq, wq), (lg, wg)):
        target[...] = source[...].astype(F32)
    queries = [wq[pl.ds(h, toks, stride=2), :].astype(BF16) for h in range(2)]
    visible = (s_id <= t_id) & (doc_row == doc_col[:, :1])
    for h in range(2):
        gap = cum_col[:, h : h + 1] - cum_row[h : h + 1, :]
        factor = jnp.where(visible, jnp.exp(jnp.where(visible, gap, 0.0)), 0.0)
        weights = (dot_nt(queries[h], keys[h].astype(BF16)) * factor).astype(BF16)
        mix[h] = dot_nn(weights, values[h])
    m_scr[...] = jnp.full_like(m_scr, LOW)
    l_scr[...] = jnp.zeros_like(l_scr)
    acc[...] = jnp.zeros_like(acc)

    for k in range(1, n_z):
        z2 = lax.rem(z + k, n_z)
        landed(s_in.at[z2], s_sem.at[z2])
    lines = [from_parts(s_in[k, 64:80, :]) for k in range(4)]
    ends = [line[:, 2:3] for line in lines]

    def weight_of(first, last, h, doc):
        total = jnp.zeros((1, 1), F32)
        for k in range(first, last + 1):
            total = total + lines[k][:, h : h + 1]
        return jnp.where(doc == ends[last], jnp.exp(total), 0.0)

    total_line = lines[0] + lines[1] + lines[2] + lines[3]
    for h in range(2):
        rows = slice(32 * h, 32 * h + 32)
        total = s_in[3, rows, :].astype(F32)
        for k in range(3):
            total = total + s_in[k, rows, :].astype(F32) * weight_of(k + 1, 3, h, ends[k])
        t_out[rows, :] = total.astype(BF16)
    t_out[64:80, :] = three_parts(jnp.where(lane == 2, ends[3], total_line))
    for d in range(1, BACK + 1):

        @pl.when(y + d < n_y)
        def _(d=d):
            send(t_out, t_in.at[d], t_snd.at[d], t_sem.at[d], {"y": y + d})

    def place(which, j):
        return which + j * (3 - 2 * which)

    def seen_here(d, zz):
        return jnp.logical_not(((d == 0) & (zz >= z)) | ((d == BACK) & (zz < z)))

    def primary(d, j):
        zz = place(half, j)
        unit = kv.at[c, 4 * d + zz]

        @pl.when(jnp.logical_not(((d == 0) & (zz == z)) | ((d == BACK) & (zz < z))))
        def _():
            landed(unit, p_sem.at[2 * d + j])

        @pl.when((y + 1 < n_y) & (d + 1 < BACK))
        def _():
            send(
                unit,
                kv.at[c, 4 * d + 4 + zz],
                a_snd.at[2 * d + j],
                p_sem.at[2 * d + 2 + j],
                {"y": lax.rem(y + 1, n_y)},
            )

        @pl.when((y + BACK < n_y) & (d == 0) & (zz >= z))
        def _():
            send(
                unit,
                kv.at[c, 4 * BACK + zz],
                a5_snd.at[j],
                p_sem.at[2 * BACK + j],
                {"y": lax.rem(y + BACK, n_y)},
            )

        @pl.when(seen_here(d, zz))
        def _():
            send(unit, unit, x_snd.at[2 * d + j], x_sem.at[2 * d + j], {"x": x_mate})
            send(unit, unit, b_snd.at[4 * d + zz], c_sem.at[4 * d + zz], {"c": c_mate})

    def secondary(d):
        for j in range(2):
            zz = place(other_half, j)
            unit = kv.at[c, 4 * d + zz]

            @pl.when(seen_here(d, zz))
            def _():
                landed(unit, x_sem.at[2 * d + j])
                send(unit, unit, b_snd.at[4 * d + zz], c_sem.at[4 * d + zz], {"c": c_mate})

    def complete(d):
        for zz in range(4):

            @pl.when(seen_here(d, zz))
            def _():
                landed(kv.at[c_mate, 4 * d + zz], c_sem.at[4 * d + zz])

    score_scale = HEAD_DIM ** (-0.5) * math.log2(math.e)
    rows_per = toks

    def attend(d, part, same_row):
        def chunk(i, carry):
            first = pl.multiple_of(i * rows_per, rows_per)
            rows = pl.ds(first, rows_per)
            query = sq[rows, :]
            query_doc = dq[rows, :][:, :1]
            line_id = lax.broadcasted_iota(jnp.int32, (rows_per, toks), 0) + first
            query_pos = lax.shift_right_logical(line_id, 1) + z * toks
            ahead = query_pos - lax.broadcasted_iota(jnp.int32, (rows_per, toks), 1)
            scores = []
            for zz in range(4):
                slot = 4 * d + zz
                tile = kv[0, slot, toks : toks + 16, :].astype(F32)
                key_doc = jnp.concatenate([tile[k : k + 1] for k in range(toks // 128)], axis=1)
                seen = key_doc == query_doc
                if same_row:
                    seen = seen & (ahead >= zz * toks)
                score = dot_nt(query, kv[0, slot, 0:toks, :])
                scores.append(jnp.where(seen, score, LOW))
            top = functools.reduce(jnp.maximum, scores)
            old_top = m_scr[rows, :][:, :1]
            new_top = jnp.maximum(old_top, jnp.max(top, axis=1, keepdims=True))
            shrink = jnp.exp2((old_top - new_top) * score_scale)
            exps = [jnp.exp2((score - new_top) * score_scale) for score in scores]
            added = jnp.sum(functools.reduce(jnp.add, exps), axis=1, keepdims=True)
            weighted = jnp.zeros((rows_per, HEAD_DIM), F32)
            for zz in range(4):
                weighted = weighted + dot_nn(exps[zz].astype(BF16), kv[1, 4 * d + zz, 0:toks, :])
            m_scr[rows, :] = jnp.broadcast_to(new_top, (rows_per, 128))
            l_scr[rows, :] = l_scr[rows, :] * shrink + added
            acc[rows, :] = acc[rows, :] * shrink + weighted
            return carry

        each = toks // rows_per
        lax.fori_loop(part * each, part * each + each, chunk, 0)

    def row_prefixes():
        run_state[...] = jnp.zeros_like(run_state)
        run_decay[...] = jnp.zeros_like(run_decay)
        pdoc[...] = jnp.full_like(pdoc, -1.0)
        for d in range(1, BACK + 1):

            @pl.when(y >= d)
            def _(d=d):
                landed(t_in.at[d], t_sem.at[d])
                line = from_parts(t_in[d, 64:80, :])
                end = line[:, 2:3]
                if d == 1:
                    pdoc[...] = jnp.broadcast_to(end, pdoc.shape)
                for h in range(2):
                    rows = slice(32 * h, 32 * h + 32)
                    passed = run_decay[0:1, h : h + 1]
                    keep = jnp.where(end == pdoc[0:1, 0:1], jnp.exp(passed), 0.0)
                    run_state[rows, :] = run_state[rows, :] + t_in[d, rows, :].astype(F32) * keep
                run_decay[...] = run_decay[...] + line

        before = pdoc[0:1, 0:1]
        for h in range(2):
            rows = slice(32 * h, 32 * h + 32)
            entry = run_state[rows, :]
            p_out[0, rows, :] = entry.astype(BF16)
            for k in range(1, 4):
                prior = entry * weight_of(0, k - 1, h, before)
                for j in range(k):
                    part = s_in[j, rows, :].astype(F32)
                    if j < k - 1:
                        part = part * weight_of(j + 1, k - 1, h, ends[j])
                    prior = prior + part
                p_out[k, rows, :] = prior.astype(BF16)
        own_doc = before
        for k in range(1, 4):
            own_doc = jnp.where(z == k, ends[k - 1], own_doc)
        pdoc[...] = jnp.broadcast_to(own_doc, pdoc.shape)
        p_in[z] = p_out[z]
        for k in range(1, n_z):
            z2 = lax.rem(z + k, n_z)
            send(p_out.at[z2], p_in.at[z], p_snd.at[k - 1], st_sem.at[z], {"z": z2})

    def carry_over():
        for k in range(1, n_z):
            z2 = lax.rem(z + k, n_z)
            landed(p_in.at[z2], st_sem.at[z2])
        opened = (dcol[...][:, :1] == pdoc[0:1, 0:1]).astype(F32)
        squares = jnp.zeros((toks, 128), F32)
        for h in range(2):
            rows = slice(32 * h, 32 * h + 32)
            state = jnp.concatenate([p_in[q, rows, :] for q in range(4)], axis=0)
            query = wq[pl.ds(h, toks, stride=2), :].astype(BF16)
            factor = jnp.exp(ccol[...][:, h : h + 1]) * opened
            mixed = mix[h] + dot_nn(query, state) * factor
            mix[h] = mixed
            squares = squares + mixed * mixed
        sums = dot_nt(jnp.ones((8, 128), F32), squares, precision=lax.Precision.HIGHEST)
        ss_in[tp] = sums[0:1, :]

    def post_squares():
        @pl.when(own_turn < n_tp - 1)
        def _():
            pl.semaphore_wait(ready, n_tp - 1 - own_turn)

        def post(k, carry):
            send(ss_in.at[tp], ss_in.at[tp], ss_snd.at[k], ss_sem.at[tp], tp_place(k))
            return carry

        lax.fori_loop(1, n_tp, post, 0)

    def finish_lin():
        def arrive(k, carry):
            t2 = lax.rem(tp + k, n_tp)
            landed(ss_in.at[t2], ss_sem.at[t2])
            return carry

        lax.fori_loop(1, n_tp, arrive, 0)
        total = jnp.sum(ss_in[...], axis=0)
        inv = lax.rsqrt(total / (n_tp * 2 * HEAD_DIM) + 1e-06)
        inv_col = as_column(inv, toks)
        for h in range(2):
            gate = wg[pl.ds(h, toks, stride=2), :]
            wo[pl.ds(h, toks, stride=2), :] = (
                mix[h] * inv_col * gain[h : h + 1, :] * jax.nn.sigmoid(gate)
            )
        lin_out[...] = wo[...].astype(BF16)

    def order(it):
        return jnp.where(it == 4, 5, jnp.where(it == 5, 4, it))

    for j in range(2):
        primary(0, j)
    post_at = jnp.where(w == 0, 4, 1)

    def step(it, carry):
        past, now, after = (order(it - 1), order(it), order(it + 1))
        has_past = (it >= 1) & (past <= y)
        for j in range(2):

            @pl.when((it < BACK) & (after <= y))
            def _(j=j):
                primary(after, j)

            if j == 0:

                @pl.when(has_past)
                def _():
                    complete(past)

            else:

                @pl.when((it <= BACK) & (now <= y))
                def _():
                    secondary(now)

                @pl.when(it == 0)
                def _():
                    row_prefixes()

                @pl.when(it == 1)
                def _():
                    carry_over()

                @pl.when(it == post_at)
                def _():
                    post_squares()

            @pl.when(has_past & (past == 0))
            def _(j=j):
                attend(past, j, True)

            @pl.when(has_past & (past > 0))
            def _(j=j):
                attend(past, j, False)

        return carry

    lax.fori_loop(0, BACK + 2, step, 0)
    soft_out[...] = (acc[...] / l_scr[...]).astype(BF16)
    finish_lin()

    for k in range(n_z - 1):
        left(s_out.at[0], s_snd.at[k])
        left(p_out.at[0], p_snd.at[k])

        @pl.when(owner)
        def _():
            left(kv.at[c, z], za_snd.at[k])

    for d in range(1, BACK + 1):

        @pl.when(y + d < n_y)
        def _(d=d):
            left(t_out, t_snd.at[d])

    def sent(k, carry):
        left(ss_in.at[tp], ss_snd.at[k])
        return carry

    lax.fori_loop(1, n_tp, sent, 0)

    def row_sent(d, carry):
        @pl.when(d <= y)
        def _():
            for j in range(2):
                zz = place(half, j)

                @pl.when((y + 1 < n_y) & (d + 1 < BACK))
                def _():
                    left(kv.at[c, 0], a_snd.at[2 * d + j])

                @pl.when((y + BACK < n_y) & (d == 0) & (zz >= z))
                def _():
                    left(kv.at[c, 0], a5_snd.at[j])

                @pl.when(seen_here(d, zz))
                def _():
                    left(kv.at[c, 0], x_snd.at[2 * d + j])

            for zz in range(4):

                @pl.when(seen_here(d, zz))
                def _():
                    left(kv.at[c, 0], b_snd.at[4 * d + zz])

        return carry

    lax.fori_loop(0, BACK + 1, row_sent, 0)


def body(sizes, lin_query, lin_key, lin_value, lin_gate, log_decay, norm_gain, doc_ids,
         soft_query, soft_key, soft_value):
    toks = lin_query.shape[0]
    n_tp = sizes[2] * sizes[3] * sizes[4]
    flat = lambda a: a.reshape(-1, HEAD_DIM)
    dma = pltpu.SemaphoreType.DMA
    rows = BACK + 1
    unit = toks + 16
    in_vmem = pl.BlockSpec(memory_space=pltpu.VMEM)
    in_place = pl.BlockSpec(memory_space=pl.ANY)
    lin_out, soft_out = pl.pallas_call(
        functools.partial(kernel, sizes),
        out_shape=(
            jax.ShapeDtypeStruct((2 * toks, HEAD_DIM), BF16),
            jax.ShapeDtypeStruct((2 * toks, HEAD_DIM), BF16),
        ),
        in_specs=[in_place] * 10,
        out_specs=(in_vmem, in_vmem),
        scratch_shapes=[
            pltpu.VMEM((2 * toks, 128), BF16),
            pltpu.VMEM((2 * toks, 128), BF16),
            pltpu.VMEM((2 * toks, 128), BF16),
            pltpu.VMEM((2 * toks, 128), BF16),
            pltpu.VMEM((2, toks), F32),
            pltpu.VMEM((2, 128), F32),
            pltpu.VMEM((1, toks), jnp.int32),
            pltpu.VMEM((2 * toks, 128), BF16),
            pltpu.VMEM((KV_HEADS * toks, 128), BF16),
            pltpu.VMEM((KV_HEADS * toks, 128), BF16),
            dma((10,)),
            pltpu.VMEM((2, 4 * rows, unit, 128), BF16),
            pltpu.VMEM((2, KV_HEADS * toks, 128), F32),
            pltpu.VMEM((2 * toks, 128), F32),
            pltpu.VMEM((2 * toks, 128), F32),
            pltpu.VMEM((2 * toks, 128), F32),
            pltpu.VMEM((2 * toks, 128), F32),
            pltpu.VMEM((2 * toks, 128), F32),
            pltpu.VMEM((8, toks), F32),
            pltpu.VMEM((toks, 8), F32),
            pltpu.VMEM((toks, 128), F32),
            pltpu.VMEM((2 * toks, 128), F32),
            pltpu.VMEM((2, toks, 128), F32),
            pltpu.VMEM((4, 80, 128), BF16),
            pltpu.VMEM((4, 80, 128), BF16),
            pltpu.VMEM((80, 128), BF16),
            pltpu.VMEM((rows, 80, 128), BF16),
            pltpu.VMEM((4, 64, 128), BF16),
            pltpu.VMEM((4, 64, 128), BF16),
            pltpu.VMEM((64, 128), F32),
            pltpu.VMEM((1, 128), F32),
            pltpu.VMEM((1, 128), F32),
            pltpu.VMEM((n_tp, 1, toks), F32),
            pltpu.VMEM((2 * toks, 128), F32),
            pltpu.VMEM((2 * toks, 128), F32),
            pltpu.VMEM((2 * toks, 128), F32),
            dma((2 * rows,)),
            dma((2 * rows,)),
            dma((4 * rows,)),
            dma((4,)),
            dma((rows,)),
            dma((4,)),
            dma((n_tp,)),
            pltpu.SemaphoreType.REGULAR,
            dma((3,)),
            dma((2 * rows,)),
            dma((2,)),
            dma((4 * rows,)),
            dma((2 * rows,)),
            dma((3,)),
            dma((rows,)),
            dma((3,)),
            dma((n_tp,)),
        ],
        compiler_params=pltpu.CompilerParams(
            collective_id=0, has_side_effects=True, vmem_limit_bytes=56 * 1024 * 1024
        ),
    )(
        flat(lin_query),
        flat(lin_key),
        flat(lin_value),
        flat(lin_gate),
        jnp.transpose(log_decay),
        norm_gain,
        doc_ids.reshape(1, toks),
        flat(soft_query),
        flat(soft_key),
        flat(soft_value),
    )
    return lin_out.reshape(toks, 2, HEAD_DIM), soft_out.reshape(toks, 2, HEAD_DIM)


def solution(mesh, sizes=(8, 4, 2, 8, 2)):
    split = Mesh(mesh.devices.reshape(sizes), ("y", "z", "w", "x", "c"))
    placed = (
        P(SEQ, TP, None),
        P(SEQ, TP, None),
        P(SEQ, TP, None),
        P(SEQ, TP, None),
        P(SEQ, TP),
        P(TP, None),
        P(SEQ),
        P(SEQ, TP, None),
        P(SEQ, None, None),
        P(SEQ, None, None),
    )
    return jax.shard_map(
        functools.partial(body, sizes),
        mesh=split,
        in_specs=placed,
        out_specs=(P(SEQ, TP, None), P(SEQ, TP, None)),
        check_vma=False,
    )
```

```python
import functools
import math

import jax
import jax.numpy as jnp
from jax import lax
from jax.experimental import pallas as pl
from jax.experimental.pallas import tpu as pltpu
from jax.sharding import Mesh
from jax.sharding import PartitionSpec as P

HEADS = 64
HEAD_DIM = 128
KV_HEADS = 8
SEQ = ("y", "z")
TP = ("w", "x", "c")
MESH = pl.DeviceIdType.MESH
F32 = jnp.float32
BF16 = jnp.bfloat16
BACK = 5
DOCS = 4
LOW = -1e30


def dot_nt(a, b, **kw):
    return lax.dot_general(a, b, (((1,), (1,)), ((), ())), preferred_element_type=F32, **kw)


def dot_tn(a, b):
    return lax.dot_general(a, b, (((0,), (0,)), ((), ())), preferred_element_type=F32)


def dot_nn(a, b):
    return lax.dot_general(a, b, (((1,), (0,)), ((), ())), preferred_element_type=F32)


def as_column(row, toks):
    return jnp.concatenate(
        [
            jnp.transpose(jnp.broadcast_to(row[:, k : k + 128], (128, 128)))
            for k in range(0, toks, 128)
        ],
        axis=0,
    )


def three_parts(line):
    high = line.astype(BF16)
    rest = line - high.astype(F32)
    middle = rest.astype(BF16)
    low = (rest - middle.astype(F32)).astype(BF16)
    row = lax.broadcasted_iota(jnp.int32, (16, 128), 0)
    parts = [jnp.broadcast_to(p.astype(F32), (16, 128)) for p in (high, middle, low)]
    return jnp.where(
        row == 0, parts[0], jnp.where(row == 1, parts[1], jnp.where(row == 2, parts[2], 0.0))
    ).astype(BF16)


def from_parts(tile):
    wide = tile.astype(F32)
    return wide[0:1] + wide[1:2] + wide[2:3]


def kernel(
    sizes,
    lq_in,
    lk_in,
    lv_in,
    lg_in,
    ld_in,
    gain_in,
    docs_in,
    sq_in,
    sk_in,
    sv_in,
    lin_out,
    soft_out,
    lq,
    lk,
    lv,
    lg,
    ld,
    gain,
    docs,
    sq,
    sk,
    sv,
    in_sem,
    kv,
    wide8,
    wq,
    wk,
    wv,
    wg,
    wo,
    dec,
    ccol,
    dcol,
    dq,
    mix,
    s_out,
    s_in,
    t_out,
    t_in,
    p_out,
    p_in,
    run_state,
    run_decay,
    pdoc,
    ss_in,
    m_scr,
    l_scr,
    acc,
    p_sem,
    x_sem,
    c_sem,
    s_sem,
    t_sem,
    st_sem,
    ss_sem,
    ready,
    za_snd,
    a_snd,
    a5_snd,
    b_snd,
    x_snd,
    s_snd,
    t_snd,
    p_snd,
    ss_snd,
):
    n_y, n_z, n_w, n_x, n_c = sizes
    n_tp = n_w * n_x * n_c
    toks = docs.shape[1]
    y, z, w = (lax.axis_index("y"), lax.axis_index("z"), lax.axis_index("w"))
    x, c = (lax.axis_index("x"), lax.axis_index("c"))
    tp = (w * n_x + x) * n_c + c
    half = lax.rem(x, 2)
    other_half = 1 - half
    x_mate = x + 1 - 2 * half
    c_mate = 1 - c
    head = (tp * 2) // (HEADS // KV_HEADS)

    def tp_place(k):
        t2 = lax.rem(tp + k, n_tp)
        return {"w": t2 // (n_x * n_c), "x": lax.rem(t2 // n_c, n_x), "c": lax.rem(t2, n_c)}

    def turn(w_, x_, c_):
        apart = jnp.minimum(x_, n_x - x_)
        step = 2 * apart - jnp.where((x_ >= 1) & (2 * x_ <= n_x), 1, 0)
        return (w_ * n_x + step) * n_c + c_

    own_turn = turn(w, x, c)
    barrier = pltpu.get_barrier_semaphore()

    def greet_tp(k, carry):
        other = tp_place(k)
        near = ((other["x"] == x) | ((other["x"] == x_mate) & (other["c"] == c))) & (other["w"] == w)

        @pl.when(near | (turn(other["w"], other["x"], other["c"]) > own_turn))
        def _():
            pl.semaphore_signal(barrier, inc=1, device_id=other, device_id_type=MESH)

        return carry

    def tell_tp(k, carry):
        other = tp_place(k)

        @pl.when(turn(other["w"], other["x"], other["c"]) < own_turn)
        def _():
            pl.semaphore_signal(ready, inc=1, device_id=other, device_id_type=MESH)

        return carry

    def greet_y(k, carry):
        pl.semaphore_signal(
            barrier, inc=1, device_id={"y": lax.rem(y + k, n_y)}, device_id_type=MESH
        )
        return carry

    loads = [
        pltpu.make_async_copy(source, target, in_sem.at[k])
        for k, (source, target) in enumerate(
            (
                (sk_in, sk),
                (sv_in, sv),
                (docs_in, docs),
                (ld_in, ld),
                (lk_in, lk),
                (lv_in, lv),
                (lq_in, lq),
                (lg_in, lg),
                (sq_in, sq),
                (gain_in, gain),
            )
        )
    ]
    for load in loads:
        load.start()
    for k in range(1, n_z):
        pl.semaphore_signal(
            barrier, inc=1, device_id={"z": lax.rem(z + k, n_z)}, device_id_type=MESH
        )
    lax.fori_loop(1, n_y, greet_y, 0)
    lax.fori_loop(1, n_tp, greet_tp, 0)

    def send(src, dst, send_sem, recv_sem, device):
        pltpu.make_async_remote_copy(
            src_ref=src,
            dst_ref=dst,
            send_sem=send_sem,
            recv_sem=recv_sem,
            device_id=device,
            device_id_type=MESH,
        ).start()

    def landed(ref, sem):
        pltpu.make_async_remote_copy(
            src_ref=ref,
            dst_ref=ref,
            send_sem=a5_snd.at[0],
            recv_sem=sem,
            device_id={"c": c_mate},
            device_id_type=MESH,
        ).wait_recv()

    def left(ref, sem):
        pltpu.make_async_remote_copy(
            src_ref=ref,
            dst_ref=ref,
            send_sem=sem,
            recv_sem=p_sem.at[0],
            device_id={"c": c_mate},
            device_id_type=MESH,
        ).wait_send()

    for load in loads[:3]:
        load.wait()
    doc_row = docs[...].astype(F32)
    for kind, source in ((0, sk), (1, sv)):
        wide8[kind] = source[...].astype(F32)
        kv[kind, z] = wide8[kind, pl.ds(head, toks, stride=KV_HEADS), :].astype(BF16)

    doc_col = as_column(doc_row, toks)
    for load in loads[3:6]:
        load.wait()
    for source, target in ((lk, wk), (lv, wv)):
        target[...] = source[...].astype(F32)

    dec[...] = jnp.zeros_like(dec)
    dec[0:2, :] = ld[...]
    t_id = lax.broadcasted_iota(jnp.int32, (toks, toks), 0)
    s_id = lax.broadcasted_iota(jnp.int32, (toks, toks), 1)
    upto = (s_id <= t_id).astype(F32)
    cum_col = dot_nt(upto, dec[...], precision=lax.Precision.HIGHEST)
    cum_row = dot_nt(dec[...], upto, precision=lax.Precision.HIGHEST)
    ccol[...] = cum_col
    last_doc = doc_row[:, toks - 1 : toks]
    tail = (doc_col[:, :1] == last_doc).astype(F32)
    keys = [wk[pl.ds(h, toks, stride=2), :] for h in range(2)]
    values = [wv[pl.ds(h, toks, stride=2), :].astype(BF16) for h in range(2)]
    decay_line = jnp.zeros((1, 128), F32)
    lane = lax.broadcasted_iota(jnp.int32, (1, 128), 1)
    for h in range(2):
        end = cum_col[toks - 1 : toks, h : h + 1]
        scale = jnp.exp(end - cum_col[:, h : h + 1]) * tail
        state = dot_tn((keys[h] * scale).astype(BF16), values[h]).astype(BF16)
        for q in range(4):
            s_out[q, 32 * h : 32 * h + 32, :] = state[32 * q : 32 * q + 32, :]
        decay_line = jnp.where(lane == h, end, decay_line)
    decay_line = jnp.where(lane == 2, last_doc, decay_line)
    for v in range(DOCS):
        count = jnp.sum((doc_row == v).astype(F32), axis=1, keepdims=True)
        decay_line = jnp.where(lane == 3 + v, count, decay_line)
    scalars = three_parts(decay_line)
    for q in range(4):
        s_out[q, 64:80, :] = scalars
    s_in[z] = s_out[z]
    for zz in range(4):
        in_half = ((zz == 0) or (zz == 3)) == (half == 0)
        for kind in range(2):

            @pl.when((zz > z) & jnp.logical_not(in_half & (c == kind)))
            def _(zz=zz, kind=kind):
                kv[kind, zz] = jnp.zeros(kv.shape[2:], BF16)

            @pl.when((zz < z) & (y >= BACK))
            def _(zz=zz, kind=kind):
                kv[kind, 4 * BACK + zz] = jnp.zeros(kv.shape[2:], BF16)

    early_mates = c + jnp.where(turn(w, x_mate, c) < own_turn, 1, 0)
    pl.semaphore_wait(barrier, (n_z - 1) + (n_y - 1) + 2 + own_turn - early_mates)

    for k in range(1, n_z):
        z2 = lax.rem(z + k, n_z)
        send(s_out.at[z2], s_in.at[z], s_snd.at[k - 1], s_sem.at[z], {"z": z2})
    owner = ((z == 0) | (z == 3)) == (half == 0)

    @pl.when(owner)
    def _():
        for k in range(1, n_z):
            z2 = lax.rem(z + jnp.where(z < 2, n_z - k, k), n_z)
            send(kv.at[c, z], kv.at[c, z], za_snd.at[k - 1], p_sem.at[z // 2], {"z": z2})

    lax.fori_loop(1, n_tp, tell_tp, 0)
    dcol[...] = doc_col
    for h in range(2):
        dq[pl.ds(h, toks, stride=2), :] = doc_col
    for load in loads[6:]:
        load.wait()
    for source, target in ((lq, wq), (lg, wg)):
        target[...] = source[...].astype(F32)
    queries = [wq[pl.ds(h, toks, stride=2), :].astype(BF16) for h in range(2)]
    visible = (s_id <= t_id) & (doc_row == doc_col[:, :1])
    for h in range(2):
        gap = cum_col[:, h : h + 1] - cum_row[h : h + 1, :]
        factor = jnp.where(visible, jnp.exp(jnp.where(visible, gap, 0.0)), 0.0)
        weights = (dot_nt(queries[h], keys[h].astype(BF16)) * factor).astype(BF16)
        mix[h] = dot_nn(weights, values[h])
    m_scr[...] = jnp.full_like(m_scr, LOW)
    l_scr[...] = jnp.zeros_like(l_scr)
    acc[...] = jnp.zeros_like(acc)

    for k in range(1, n_z):
        z2 = lax.rem(z + k, n_z)
        landed(s_in.at[z2], s_sem.at[z2])
    lines = [from_parts(s_in[k, 64:80, :]) for k in range(4)]
    ends = [line[:, 2:3] for line in lines]

    def weight_of(first, last, h, doc):
        total = jnp.zeros((1, 1), F32)
        for k in range(first, last + 1):
            total = total + lines[k][:, h : h + 1]
        return jnp.where(doc == ends[last], jnp.exp(total), 0.0)

    total_line = lines[0] + lines[1] + lines[2] + lines[3]
    for h in range(2):
        rows = slice(32 * h, 32 * h + 32)
        total = s_in[3, rows, :].astype(F32)
        for k in range(3):
            total = total + s_in[k, rows, :].astype(F32) * weight_of(k + 1, 3, h, ends[k])
        t_out[rows, :] = total.astype(BF16)
    t_out[64:80, :] = three_parts(jnp.where(lane == 2, ends[3], total_line))
    for d in range(1, BACK + 1):

        @pl.when(y + d < n_y)
        def _(d=d):
            send(t_out, t_in.at[d], t_snd.at[d], t_sem.at[d], {"y": y + d})

    def place(which, j):
        return which + j * (3 - 2 * which)

    def seen_here(d, zz):
        return jnp.logical_not(((d == 0) & (zz >= z)) | ((d == BACK) & (zz < z)))

    def primary(d, j):
        zz = place(half, j)
        unit = kv.at[c, 4 * d + zz]

        @pl.when(jnp.logical_not(((d == 0) & (zz == z)) | ((d == BACK) & (zz < z))))
        def _():
            landed(unit, p_sem.at[2 * d + j])

        @pl.when((y + 1 < n_y) & (d + 1 < BACK))
        def _():
            send(
                unit,
                kv.at[c, 4 * d + 4 + zz],
                a_snd.at[2 * d + j],
                p_sem.at[2 * d + 2 + j],
                {"y": lax.rem(y + 1, n_y)},
            )

        @pl.when((y + BACK < n_y) & (d == 0) & (zz >= z))
        def _():
            send(
                unit,
                kv.at[c, 4 * BACK + zz],
                a5_snd.at[j],
                p_sem.at[2 * BACK + j],
                {"y": lax.rem(y + BACK, n_y)},
            )

        @pl.when(seen_here(d, zz))
        def _():
            send(unit, unit, x_snd.at[2 * d + j], x_sem.at[2 * d + j], {"x": x_mate})
            send(unit, unit, b_snd.at[4 * d + zz], c_sem.at[4 * d + zz], {"c": c_mate})

    def secondary(d):
        for j in range(2):
            zz = place(other_half, j)
            unit = kv.at[c, 4 * d + zz]

            @pl.when(seen_here(d, zz))
            def _():
                landed(unit, x_sem.at[2 * d + j])
                send(unit, unit, b_snd.at[4 * d + zz], c_sem.at[4 * d + zz], {"c": c_mate})

    def complete(d):
        for zz in range(4):

            @pl.when(seen_here(d, zz))
            def _():
                landed(kv.at[c_mate, 4 * d + zz], c_sem.at[4 * d + zz])

    score_scale = HEAD_DIM ** (-0.5) * math.log2(math.e)
    rows_per = toks

    def attend(d, part, same_row):
        def chunk(i, carry):
            first = pl.multiple_of(i * rows_per, rows_per)
            rows = pl.ds(first, rows_per)
            query = sq[rows, :]
            key_id = lax.broadcasted_iota(jnp.int32, (rows_per, toks), 1)
            inside = key_id.astype(F32) - dq[rows, :][:, :1]
            line_id = lax.broadcasted_iota(jnp.int32, (rows_per, toks), 0) + first
            query_pos = lax.shift_right_logical(line_id, 1) + z * toks
            ahead = query_pos - key_id
            scores = []
            for zz in range(4):
                slot = 4 * d + zz
                seen = inside >= ((4 * d - zz) * toks).astype(F32)
                if same_row:
                    seen = seen & (ahead >= zz * toks)
                score = dot_nt(query, kv[0, slot])
                scores.append(jnp.where(seen, score, LOW))
            top = functools.reduce(jnp.maximum, scores)
            old_top = m_scr[rows, :][:, :1]
            new_top = jnp.maximum(old_top, jnp.max(top, axis=1, keepdims=True))
            shrink = jnp.exp2((old_top - new_top) * score_scale)
            exps = [jnp.exp2((score - new_top) * score_scale) for score in scores]
            added = jnp.sum(functools.reduce(jnp.add, exps), axis=1, keepdims=True)
            weighted = jnp.zeros((rows_per, HEAD_DIM), F32)
            for zz in range(4):
                weighted = weighted + dot_nn(exps[zz].astype(BF16), kv[1, 4 * d + zz])
            m_scr[rows, :] = jnp.broadcast_to(new_top, (rows_per, 128))
            l_scr[rows, :] = l_scr[rows, :] * shrink + added
            acc[rows, :] = acc[rows, :] * shrink + weighted
            return carry

        each = toks // rows_per
        lax.fori_loop(part * each, part * each + each, chunk, 0)

    def row_prefixes():
        run_state[...] = jnp.zeros_like(run_state)
        run_decay[...] = jnp.zeros_like(run_decay)
        pdoc[...] = jnp.full_like(pdoc, -1.0)
        for d in range(1, BACK + 1):

            @pl.when(y >= d)
            def _(d=d):
                landed(t_in.at[d], t_sem.at[d])
                line = from_parts(t_in[d, 64:80, :])
                end = line[:, 2:3]
                if d == 1:
                    pdoc[...] = jnp.broadcast_to(end, pdoc.shape)
                for h in range(2):
                    rows = slice(32 * h, 32 * h + 32)
                    passed = run_decay[0:1, h : h + 1]
                    keep = jnp.where(end == pdoc[0:1, 0:1], jnp.exp(passed), 0.0)
                    run_state[rows, :] = run_state[rows, :] + t_in[d, rows, :].astype(F32) * keep
                run_decay[...] = run_decay[...] + line

        before = pdoc[0:1, 0:1]
        for h in range(2):
            rows = slice(32 * h, 32 * h + 32)
            entry = run_state[rows, :]
            p_out[0, rows, :] = entry.astype(BF16)
            for k in range(1, 4):
                prior = entry * weight_of(0, k - 1, h, before)
                for j in range(k):
                    part = s_in[j, rows, :].astype(F32)
                    if j < k - 1:
                        part = part * weight_of(j + 1, k - 1, h, ends[j])
                    prior = prior + part
                p_out[k, rows, :] = prior.astype(BF16)
        began = jnp.zeros((1, 1), F32)
        starts = jnp.zeros(dq.shape, F32)
        for v in range(DOCS):
            earlier = run_decay[0:1, 3 + v : 4 + v]
            first = jnp.where(earlier > 0, -earlier, began)
            starts = jnp.where(dq[...] == v, first, starts)
            began = began + total_line[:, 3 + v : 4 + v]
        dq[...] = starts
        own_doc = before
        for k in range(1, 4):
            own_doc = jnp.where(z == k, ends[k - 1], own_doc)
        pdoc[...] = jnp.broadcast_to(own_doc, pdoc.shape)
        p_in[z] = p_out[z]
        for k in range(1, n_z):
            z2 = lax.rem(z + k, n_z)
            send(p_out.at[z2], p_in.at[z], p_snd.at[k - 1], st_sem.at[z], {"z": z2})

    def carry_over():
        for k in range(1, n_z):
            z2 = lax.rem(z + k, n_z)
            landed(p_in.at[z2], st_sem.at[z2])
        opened = (dcol[...][:, :1] == pdoc[0:1, 0:1]).astype(F32)
        squares = jnp.zeros((toks, 128), F32)
        for h in range(2):
            rows = slice(32 * h, 32 * h + 32)
            state = jnp.concatenate([p_in[q, rows, :] for q in range(4)], axis=0)
            query = wq[pl.ds(h, toks, stride=2), :].astype(BF16)
            factor = jnp.exp(ccol[...][:, h : h + 1]) * opened
            mixed = mix[h] + dot_nn(query, state) * factor
            mix[h] = mixed
            squares = squares + mixed * mixed
        sums = dot_nt(jnp.ones((8, 128), F32), squares, precision=lax.Precision.HIGHEST)
        ss_in[tp] = sums[0:1, :]

    def post_squares():
        @pl.when(own_turn < n_tp - 1)
        def _():
            pl.semaphore_wait(ready, n_tp - 1 - own_turn)

        def post(k, carry):
            send(ss_in.at[tp], ss_in.at[tp], ss_snd.at[k], ss_sem.at[tp], tp_place(k))
            return carry

        lax.fori_loop(1, n_tp, post, 0)

    def finish_lin():
        def arrive(k, carry):
            t2 = lax.rem(tp + k, n_tp)
            landed(ss_in.at[t2], ss_sem.at[t2])
            return carry

        lax.fori_loop(1, n_tp, arrive, 0)
        total = jnp.sum(ss_in[...], axis=0)
        inv = lax.rsqrt(total / (n_tp * 2 * HEAD_DIM) + 1e-06)
        inv_col = as_column(inv, toks)
        for h in range(2):
            wo[pl.ds(h, toks, stride=2), :] = mix[h] * inv_col
        lin_out[...] = wo[...].astype(BF16)

    def order(it):
        return jnp.where(it == 4, 5, jnp.where(it == 5, 4, it))

    for j in range(2):
        primary(0, j)
    post_at = jnp.where(w == 0, 4, 1)

    def step(it, carry):
        past, now, after = (order(it - 1), order(it), order(it + 1))
        has_past = (it >= 1) & (past <= y)
        for j in range(2):

            @pl.when((it < BACK) & (after <= y))
            def _(j=j):
                primary(after, j)

            if j == 0:

                @pl.when(has_past)
                def _():
                    complete(past)

            else:

                @pl.when((it <= BACK) & (now <= y))
                def _():
                    secondary(now)

                @pl.when(it == 0)
                def _():
                    row_prefixes()

                @pl.when(it == 1)
                def _():
                    carry_over()

                @pl.when(it == post_at)
                def _():
                    post_squares()

            @pl.when(has_past & (past == 0))
            def _(j=j):
                attend(past, j, True)

            @pl.when(has_past & (past > 0))
            def _(j=j):
                attend(past, j, False)

        return carry

    lax.fori_loop(0, BACK + 2, step, 0)
    soft_out[...] = (acc[...] / l_scr[...]).astype(BF16)
    for h in range(2):
        gate = wg[pl.ds(h, toks, stride=2), :]
        mix[h] = mix[h] * gain[h : h + 1, :] * jax.nn.sigmoid(gate)

    for k in range(n_z - 1):
        left(s_out.at[0], s_snd.at[k])
        left(p_out.at[0], p_snd.at[k])

        @pl.when(owner)
        def _():
            left(kv.at[c, z], za_snd.at[k])

    for d in range(1, BACK + 1):

        @pl.when(y + d < n_y)
        def _(d=d):
            left(t_out, t_snd.at[d])

    def sent(k, carry):
        left(ss_in.at[tp], ss_snd.at[k])
        return carry

    lax.fori_loop(1, n_tp, sent, 0)

    def row_sent(d, carry):
        @pl.when(d <= y)
        def _():
            for j in range(2):
                zz = place(half, j)

                @pl.when((y + 1 < n_y) & (d + 1 < BACK))
                def _():
                    left(kv.at[c, 0], a_snd.at[2 * d + j])

                @pl.when((y + BACK < n_y) & (d == 0) & (zz >= z))
                def _():
                    left(kv.at[c, 0], a5_snd.at[j])

                @pl.when(seen_here(d, zz))
                def _():
                    left(kv.at[c, 0], x_snd.at[2 * d + j])

            for zz in range(4):

                @pl.when(seen_here(d, zz))
                def _():
                    left(kv.at[c, 0], b_snd.at[4 * d + zz])

        return carry

    lax.fori_loop(0, BACK + 1, row_sent, 0)
    finish_lin()


def hand_over(lin, soft, lin_out, soft_out, sem):
    copies = [
        pltpu.make_async_copy(lin, lin_out, sem.at[0]),
        pltpu.make_async_copy(soft, soft_out, sem.at[1]),
    ]
    for copy in copies:
        copy.start()
    for copy in copies:
        copy.wait()


def body(sizes, lin_query, lin_key, lin_value, lin_gate, log_decay, norm_gain, doc_ids,
         soft_query, soft_key, soft_value):
    toks = lin_query.shape[0]
    n_tp = sizes[2] * sizes[3] * sizes[4]
    flat = lambda a: a.reshape(-1, HEAD_DIM)
    dma = pltpu.SemaphoreType.DMA
    rows = BACK + 1
    in_vmem = pl.BlockSpec(memory_space=pltpu.VMEM)
    in_place = pl.BlockSpec(memory_space=pl.ANY)
    lin_out, soft_out = pl.pallas_call(
        functools.partial(kernel, sizes),
        out_shape=(
            pltpu.VMEM((2 * toks, HEAD_DIM), BF16),
            pltpu.VMEM((2 * toks, HEAD_DIM), BF16),
        ),
        in_specs=[in_place] * 10,
        out_specs=(in_vmem, in_vmem),
        scratch_shapes=[
            pltpu.VMEM((2 * toks, 128), BF16),
            pltpu.VMEM((2 * toks, 128), BF16),
            pltpu.VMEM((2 * toks, 128), BF16),
            pltpu.VMEM((2 * toks, 128), BF16),
            pltpu.VMEM((2, toks), F32),
            pltpu.VMEM((2, 128), F32),
            pltpu.VMEM((1, toks), jnp.int32),
            pltpu.VMEM((2 * toks, 128), BF16),
            pltpu.VMEM((KV_HEADS * toks, 128), BF16),
            pltpu.VMEM((KV_HEADS * toks, 128), BF16),
            dma((10,)),
            pltpu.VMEM((2, 4 * rows, toks, 128), BF16),
            pltpu.VMEM((2, KV_HEADS * toks, 128), F32),
            pltpu.VMEM((2 * toks, 128), F32),
            pltpu.VMEM((2 * toks, 128), F32),
            pltpu.VMEM((2 * toks, 128), F32),
            pltpu.VMEM((2 * toks, 128), F32),
            pltpu.VMEM((2 * toks, 128), F32),
            pltpu.VMEM((8, toks), F32),
            pltpu.VMEM((toks, 8), F32),
            pltpu.VMEM((toks, 128), F32),
            pltpu.VMEM((2 * toks, 128), F32),
            pltpu.VMEM((2, toks, 128), F32),
            pltpu.VMEM((4, 80, 128), BF16),
            pltpu.VMEM((4, 80, 128), BF16),
            pltpu.VMEM((80, 128), BF16),
            pltpu.VMEM((rows, 80, 128), BF16),
            pltpu.VMEM((4, 64, 128), BF16),
            pltpu.VMEM((4, 64, 128), BF16),
            pltpu.VMEM((64, 128), F32),
            pltpu.VMEM((1, 128), F32),
            pltpu.VMEM((1, 128), F32),
            pltpu.VMEM((n_tp, 1, toks), F32),
            pltpu.VMEM((2 * toks, 128), F32),
            pltpu.VMEM((2 * toks, 128), F32),
            pltpu.VMEM((2 * toks, 128), F32),
            dma((2 * rows,)),
            dma((2 * rows,)),
            dma((4 * rows,)),
            dma((4,)),
            dma((rows,)),
            dma((4,)),
            dma((n_tp,)),
            pltpu.SemaphoreType.REGULAR,
            dma((3,)),
            dma((2 * rows,)),
            dma((2,)),
            dma((4 * rows,)),
            dma((2 * rows,)),
            dma((3,)),
            dma((rows,)),
            dma((3,)),
            dma((n_tp,)),
        ],
        compiler_params=pltpu.CompilerParams(
            collective_id=0, has_side_effects=True, vmem_limit_bytes=56 * 1024 * 1024
        ),
    )(
        flat(lin_query),
        flat(lin_key),
        flat(lin_value),
        flat(lin_gate),
        jnp.transpose(log_decay),
        norm_gain,
        doc_ids.reshape(1, toks),
        flat(soft_query),
        flat(soft_key),
        flat(soft_value),
    )
    lin_out, soft_out = pl.pallas_call(
        hand_over,
        out_shape=(
            jax.ShapeDtypeStruct((2 * toks, HEAD_DIM), BF16),
            jax.ShapeDtypeStruct((2 * toks, HEAD_DIM), BF16),
        ),
        in_specs=[in_vmem] * 2,
        out_specs=(in_place, in_place),
        scratch_shapes=[dma((2,))],
        compiler_params=pltpu.CompilerParams(vmem_limit_bytes=8 * 1024 * 1024),
    )(lin_out, soft_out)
    return lin_out.reshape(toks, 2, HEAD_DIM), soft_out.reshape(toks, 2, HEAD_DIM)


def solution(mesh, sizes=(8, 4, 2, 8, 2)):
    split = Mesh(mesh.devices.reshape(sizes), ("y", "z", "w", "x", "c"))
    placed = (
        P(SEQ, TP, None),
        P(SEQ, TP, None),
        P(SEQ, TP, None),
        P(SEQ, TP, None),
        P(SEQ, TP),
        P(TP, None),
        P(SEQ),
        P(SEQ, TP, None),
        P(SEQ, None, None),
        P(SEQ, None, None),
    )
    return jax.shard_map(
        functools.partial(body, sizes),
        mesh=split,
        in_specs=placed,
        out_specs=(P(SEQ, TP, None), P(SEQ, TP, None)),
        check_vma=False,
    )
```

```python
import functools
import math

import jax
import jax.numpy as jnp
from jax import lax
from jax.experimental import pallas as pl
from jax.experimental.pallas import tpu as pltpu
from jax.sharding import Mesh
from jax.sharding import PartitionSpec as P

HEADS = 64
HEAD_DIM = 128
KV_HEADS = 8
SEQ = ("y", "z")
TP = ("w", "x", "c")
MESH = pl.DeviceIdType.MESH
F32 = jnp.float32
BF16 = jnp.bfloat16
BACK = 5
DOCS = 4
LOW = -1e30


def dot_nt(a, b, **kw):
    return lax.dot_general(a, b, (((1,), (1,)), ((), ())), preferred_element_type=F32, **kw)


def dot_tn(a, b):
    return lax.dot_general(a, b, (((0,), (0,)), ((), ())), preferred_element_type=F32)


def dot_nn(a, b):
    return lax.dot_general(a, b, (((1,), (0,)), ((), ())), preferred_element_type=F32)


def as_column(row, toks):
    return jnp.concatenate(
        [
            jnp.transpose(jnp.broadcast_to(row[:, k : k + 128], (128, 128)))
            for k in range(0, toks, 128)
        ],
        axis=0,
    )


def three_parts(line):
    high = line.astype(BF16)
    rest = line - high.astype(F32)
    middle = rest.astype(BF16)
    low = (rest - middle.astype(F32)).astype(BF16)
    row = lax.broadcasted_iota(jnp.int32, (16, 128), 0)
    parts = [jnp.broadcast_to(p.astype(F32), (16, 128)) for p in (high, middle, low)]
    return jnp.where(
        row == 0, parts[0], jnp.where(row == 1, parts[1], jnp.where(row == 2, parts[2], 0.0))
    ).astype(BF16)


def from_parts(tile):
    wide = tile.astype(F32)
    return wide[0:1] + wide[1:2] + wide[2:3]


def kernel(
    sizes,
    lq_in,
    lk_in,
    lv_in,
    lg_in,
    ld_in,
    gain_in,
    docs_in,
    sq_in,
    sk_in,
    sv_in,
    lin_out,
    soft_out,
    lq,
    lk,
    lv,
    lg,
    ld,
    gain,
    docs,
    sq,
    sk,
    sv,
    in_sem,
    kv,
    wide8,
    wq,
    wk,
    wv,
    wg,
    wo,
    dec,
    ccol,
    dcol,
    dq,
    mix,
    s_out,
    s_in,
    t_out,
    t_in,
    p_out,
    p_in,
    run_state,
    run_decay,
    pdoc,
    ss_in,
    m_scr,
    l_scr,
    acc,
    p_sem,
    x_sem,
    c_sem,
    s_sem,
    t_sem,
    st_sem,
    ss_sem,
    ready,
    za_snd,
    a_snd,
    a5_snd,
    b_snd,
    x_snd,
    s_snd,
    t_snd,
    p_snd,
    ss_snd,
):
    n_y, n_z, n_w, n_x, n_c = sizes
    n_tp = n_w * n_x * n_c
    toks = docs.shape[1]
    y, z, w = (lax.axis_index("y"), lax.axis_index("z"), lax.axis_index("w"))
    x, c = (lax.axis_index("x"), lax.axis_index("c"))
    tp = (w * n_x + x) * n_c + c
    half = lax.rem(x, 2)
    other_half = 1 - half
    x_mate = x + 1 - 2 * half
    c_mate = 1 - c
    head = (tp * 2) // (HEADS // KV_HEADS)

    n_xc = n_x * n_c

    def tp_place(k):
        away = k <= n_tp - n_xc
        w2 = lax.rem(w + jnp.where(away, 1, 0), n_w)
        xc2 = lax.rem(x * n_c + c + k - jnp.where(away, 1, n_tp - n_xc), n_xc)
        return {"w": w2, "x": xc2 // n_c, "c": lax.rem(xc2, n_c)}

    def turn(w_, x_, c_):
        apart = jnp.minimum(x_, n_x - x_)
        step = 2 * apart - jnp.where((x_ >= 1) & (2 * x_ <= n_x), 1, 0)
        return (w_ * n_x + step) * n_c + c_

    own_turn = turn(w, x, c)
    barrier = pltpu.get_barrier_semaphore()

    def at_turn(t):
        step = lax.rem(t, n_xc) // n_c
        x2 = jnp.where(lax.rem(step, 2) == 1, (step + 1) // 2, n_x - step // 2)
        return {"w": t // n_xc, "x": lax.rem(x2, n_x), "c": lax.rem(t, n_c)}

    def greet_tp(t, carry):
        pl.semaphore_signal(barrier, inc=1, device_id=at_turn(t), device_id_type=MESH)
        return carry

    def tell_tp(t, carry):
        pl.semaphore_signal(ready, inc=1, device_id=at_turn(t), device_id_type=MESH)
        return carry

    def greet_y(k, carry):
        pl.semaphore_signal(
            barrier, inc=1, device_id={"y": lax.rem(y + k, n_y)}, device_id_type=MESH
        )
        return carry

    loads = [
        pltpu.make_async_copy(source, target, in_sem.at[k])
        for k, (source, target) in enumerate(
            (
                (docs_in, docs),
                (ld_in, ld),
                (lk_in, lk),
                (lv_in, lv),
                (sk_in, sk),
                (sv_in, sv),
                (lq_in, lq),
                (lg_in, lg),
                (sq_in, sq),
                (gain_in, gain),
            )
        )
    ]
    for load in loads:
        load.start()
    for k in range(1, n_z):
        pl.semaphore_signal(
            barrier, inc=1, device_id={"z": lax.rem(z + k, n_z)}, device_id_type=MESH
        )
    lax.fori_loop(1, n_y, greet_y, 0)

    @pl.when(c == 1)
    def _():
        pl.semaphore_signal(barrier, inc=1, device_id={"c": c_mate}, device_id_type=MESH)

    @pl.when(turn(w, x_mate, c) < own_turn)
    def _():
        pl.semaphore_signal(barrier, inc=1, device_id={"x": x_mate}, device_id_type=MESH)

    lax.fori_loop(own_turn + 1, n_tp, greet_tp, 0)

    def send(src, dst, send_sem, recv_sem, device):
        pltpu.make_async_remote_copy(
            src_ref=src,
            dst_ref=dst,
            send_sem=send_sem,
            recv_sem=recv_sem,
            device_id=device,
            device_id_type=MESH,
        ).start()

    def landed(ref, sem):
        pltpu.make_async_remote_copy(
            src_ref=ref,
            dst_ref=ref,
            send_sem=a5_snd.at[0],
            recv_sem=sem,
            device_id={"c": c_mate},
            device_id_type=MESH,
        ).wait_recv()

    def left(ref, sem):
        pltpu.make_async_remote_copy(
            src_ref=ref,
            dst_ref=ref,
            send_sem=sem,
            recv_sem=p_sem.at[0],
            device_id={"c": c_mate},
            device_id_type=MESH,
        ).wait_send()

    for load in loads[:4]:
        load.wait()
    doc_row = docs[...].astype(F32)
    doc_col = as_column(doc_row, toks)
    for source, target in ((lk, wk), (lv, wv)):
        target[...] = source[...].astype(F32)

    dec[...] = jnp.zeros_like(dec)
    dec[0:2, :] = ld[...]
    t_id = lax.broadcasted_iota(jnp.int32, (toks, toks), 0)
    s_id = lax.broadcasted_iota(jnp.int32, (toks, toks), 1)
    upto = (s_id <= t_id).astype(F32)
    cum_col = dot_nt(upto, dec[...], precision=lax.Precision.HIGHEST)
    cum_row = dot_nt(dec[...], upto, precision=lax.Precision.HIGHEST)
    ccol[...] = cum_col
    last_doc = doc_row[:, toks - 1 : toks]
    tail = (doc_col[:, :1] == last_doc).astype(F32)
    keys = [wk[pl.ds(h, toks, stride=2), :] for h in range(2)]
    values = [wv[pl.ds(h, toks, stride=2), :].astype(BF16) for h in range(2)]
    decay_line = jnp.zeros((1, 128), F32)
    lane = lax.broadcasted_iota(jnp.int32, (1, 128), 1)
    for h in range(2):
        end = cum_col[toks - 1 : toks, h : h + 1]
        scale = jnp.exp(end - cum_col[:, h : h + 1]) * tail
        state = dot_tn((keys[h] * scale).astype(BF16), values[h]).astype(BF16)
        for q in range(4):
            s_out[q, 32 * h : 32 * h + 32, :] = state[32 * q : 32 * q + 32, :]
        decay_line = jnp.where(lane == h, end, decay_line)
    decay_line = jnp.where(lane == 2, last_doc, decay_line)
    for v in range(DOCS):
        count = jnp.sum((doc_row == v).astype(F32), axis=1, keepdims=True)
        decay_line = jnp.where(lane == 3 + v, count, decay_line)
    scalars = three_parts(decay_line)
    for q in range(4):
        s_out[q, 64:80, :] = scalars
    s_in[z] = s_out[z]
    early_mates = c + jnp.where(turn(w, x_mate, c) < own_turn, 1, 0)

    def greeted_and_sent():
        pl.semaphore_wait(barrier, (n_z - 1) + (n_y - 1) + 2 + own_turn - early_mates)

        for k in range(1, n_z):
            z2 = lax.rem(z + k, n_z)
            send(s_out.at[z2], s_in.at[z], s_snd.at[k - 1], s_sem.at[z], {"z": z2})

    late = w == 1

    @pl.when(late)
    def _():
        greeted_and_sent()

    for load in loads[4:6]:
        load.wait()
    for kind, source in ((0, sk), (1, sv)):
        wide8[kind] = source[...].astype(F32)
        kv[kind, z] = wide8[kind, pl.ds(head, toks, stride=KV_HEADS), :].astype(BF16)

    for zz in range(4):
        in_half = ((zz == 0) or (zz == 3)) == (half == 0)
        for kind in range(2):

            @pl.when((zz > z) & jnp.logical_not(in_half & (c == kind)))
            def _(zz=zz, kind=kind):
                kv[kind, zz] = jnp.zeros(kv.shape[2:], BF16)

            @pl.when((zz < z) & (y >= BACK))
            def _(zz=zz, kind=kind):
                kv[kind, 4 * BACK + zz] = jnp.zeros(kv.shape[2:], BF16)

    @pl.when(jnp.logical_not(late))
    def _():
        greeted_and_sent()

    owner = ((z == 0) | (z == 3)) == (half == 0)

    @pl.when(owner)
    def _():
        for k in range(1, n_z):
            z2 = lax.rem(z + jnp.where(z < 2, n_z - k, k), n_z)
            send(kv.at[c, z], kv.at[c, z], za_snd.at[k - 1], p_sem.at[z // 2], {"z": z2})

    lax.fori_loop(0, own_turn, tell_tp, 0)
    dcol[...] = doc_col
    for h in range(2):
        dq[pl.ds(h, toks, stride=2), :] = doc_col
    for load in loads[6:]:
        load.wait()
    for source, target in ((lq, wq), (lg, wg)):
        target[...] = source[...].astype(F32)
    queries = [wq[pl.ds(h, toks, stride=2), :].astype(BF16) for h in range(2)]
    visible = (s_id <= t_id) & (doc_row == doc_col[:, :1])
    for h in range(2):
        gap = cum_col[:, h : h + 1] - cum_row[h : h + 1, :]
        factor = jnp.where(visible, jnp.exp(jnp.where(visible, gap, 0.0)), 0.0)
        weights = (dot_nt(queries[h], keys[h].astype(BF16)) * factor).astype(BF16)
        mix[h] = dot_nn(weights, values[h])
    m_scr[...] = jnp.full_like(m_scr, LOW)
    l_scr[...] = jnp.zeros_like(l_scr)
    acc[...] = jnp.zeros_like(acc)

    for k in range(1, n_z):
        z2 = lax.rem(z + k, n_z)
        landed(s_in.at[z2], s_sem.at[z2])
    lines = [from_parts(s_in[k, 64:80, :]) for k in range(4)]
    ends = [line[:, 2:3] for line in lines]

    def weight_of(first, last, h, doc):
        total = jnp.zeros((1, 1), F32)
        for k in range(first, last + 1):
            total = total + lines[k][:, h : h + 1]
        return jnp.where(doc == ends[last], jnp.exp(total), 0.0)

    total_line = lines[0] + lines[1] + lines[2] + lines[3]
    for h in range(2):
        rows = slice(32 * h, 32 * h + 32)
        total = s_in[3, rows, :].astype(F32)
        for k in range(3):
            total = total + s_in[k, rows, :].astype(F32) * weight_of(k + 1, 3, h, ends[k])
        t_out[rows, :] = total.astype(BF16)
    t_out[64:80, :] = three_parts(jnp.where(lane == 2, ends[3], total_line))
    for d in range(1, BACK + 1):

        @pl.when(y + d < n_y)
        def _(d=d):
            send(t_out, t_in.at[d], t_snd.at[d], t_sem.at[d], {"y": y + d})

    def place(which, j):
        return which + j * (3 - 2 * which)

    def seen_here(d, zz):
        return jnp.logical_not(((d == 0) & (zz >= z)) | ((d == BACK) & (zz < z)))

    def primary(d, j):
        zz = place(half, j)
        unit = kv.at[c, 4 * d + zz]

        @pl.when(jnp.logical_not(((d == 0) & (zz == z)) | ((d == BACK) & (zz < z))))
        def _():
            landed(unit, p_sem.at[2 * d + j])

        @pl.when((y + 1 < n_y) & (d + 1 < BACK))
        def _():
            send(
                unit,
                kv.at[c, 4 * d + 4 + zz],
                a_snd.at[2 * d + j],
                p_sem.at[2 * d + 2 + j],
                {"y": lax.rem(y + 1, n_y)},
            )

        @pl.when((y + BACK < n_y) & (d == 0) & (zz >= z))
        def _():
            send(
                unit,
                kv.at[c, 4 * BACK + zz],
                a5_snd.at[j],
                p_sem.at[2 * BACK + j],
                {"y": lax.rem(y + BACK, n_y)},
            )

        @pl.when(seen_here(d, zz))
        def _():
            send(unit, unit, x_snd.at[2 * d + j], x_sem.at[2 * d + j], {"x": x_mate})
            send(unit, unit, b_snd.at[4 * d + zz], c_sem.at[4 * d + zz], {"c": c_mate})

    def secondary(d):
        for j in range(2):
            zz = place(other_half, j)
            unit = kv.at[c, 4 * d + zz]

            @pl.when(seen_here(d, zz))
            def _():
                landed(unit, x_sem.at[2 * d + j])
                send(unit, unit, b_snd.at[4 * d + zz], c_sem.at[4 * d + zz], {"c": c_mate})

    def complete(d):
        for zz in range(4):

            @pl.when(seen_here(d, zz))
            def _():
                landed(kv.at[c_mate, 4 * d + zz], c_sem.at[4 * d + zz])

    score_scale = HEAD_DIM ** (-0.5) * math.log2(math.e)
    rows_per = toks

    def attend(d, part, same_row):
        def chunk(i, carry):
            first = pl.multiple_of(i * rows_per, rows_per)
            rows = pl.ds(first, rows_per)
            query = sq[rows, :]
            key_id = lax.broadcasted_iota(jnp.int32, (rows_per, toks), 1)
            inside = key_id.astype(F32) - dq[rows, :][:, :1]
            line_id = lax.broadcasted_iota(jnp.int32, (rows_per, toks), 0) + first
            query_pos = lax.shift_right_logical(line_id, 1) + z * toks
            ahead = query_pos - key_id
            scores = []
            for zz in range(4):
                slot = 4 * d + zz
                seen = inside >= ((4 * d - zz) * toks).astype(F32)
                if same_row:
                    seen = seen & (ahead >= zz * toks)
                score = dot_nt(query, kv[0, slot])
                scores.append(jnp.where(seen, score, LOW))
            top = functools.reduce(jnp.maximum, scores)
            old_top = m_scr[rows, :][:, :1]
            new_top = jnp.maximum(old_top, jnp.max(top, axis=1, keepdims=True))
            shrink = jnp.exp2((old_top - new_top) * score_scale)
            exps = [jnp.exp2((score - new_top) * score_scale) for score in scores]
            added = jnp.sum(functools.reduce(jnp.add, exps), axis=1, keepdims=True)
            weighted = jnp.zeros((rows_per, HEAD_DIM), F32)
            for zz in range(4):
                weighted = weighted + dot_nn(exps[zz].astype(BF16), kv[1, 4 * d + zz])
            m_scr[rows, :] = jnp.broadcast_to(new_top, (rows_per, 128))
            l_scr[rows, :] = l_scr[rows, :] * shrink + added
            acc[rows, :] = acc[rows, :] * shrink + weighted
            return carry

        each = toks // rows_per
        lax.fori_loop(part * each, part * each + each, chunk, 0)

    def row_prefixes():
        run_state[...] = jnp.zeros_like(run_state)
        run_decay[...] = jnp.zeros_like(run_decay)
        pdoc[...] = jnp.full_like(pdoc, -1.0)
        for d in range(1, BACK + 1):

            @pl.when(y >= d)
            def _(d=d):
                landed(t_in.at[d], t_sem.at[d])
                line = from_parts(t_in[d, 64:80, :])
                end = line[:, 2:3]
                if d == 1:
                    pdoc[...] = jnp.broadcast_to(end, pdoc.shape)
                for h in range(2):
                    rows = slice(32 * h, 32 * h + 32)
                    passed = run_decay[0:1, h : h + 1]
                    keep = jnp.where(end == pdoc[0:1, 0:1], jnp.exp(passed), 0.0)
                    run_state[rows, :] = run_state[rows, :] + t_in[d, rows, :].astype(F32) * keep
                run_decay[...] = run_decay[...] + line

        before = pdoc[0:1, 0:1]
        for h in range(2):
            rows = slice(32 * h, 32 * h + 32)
            entry = run_state[rows, :]
            p_out[0, rows, :] = entry.astype(BF16)
            for k in range(1, 4):
                prior = entry * weight_of(0, k - 1, h, before)
                for j in range(k):
                    part = s_in[j, rows, :].astype(F32)
                    if j < k - 1:
                        part = part * weight_of(j + 1, k - 1, h, ends[j])
                    prior = prior + part
                p_out[k, rows, :] = prior.astype(BF16)
        began = jnp.zeros((1, 1), F32)
        starts = jnp.zeros(dq.shape, F32)
        for v in range(DOCS):
            earlier = run_decay[0:1, 3 + v : 4 + v]
            first = jnp.where(earlier > 0, -earlier, began)
            starts = jnp.where(dq[...] == v, first, starts)
            began = began + total_line[:, 3 + v : 4 + v]
        dq[...] = starts
        own_doc = before
        for k in range(1, 4):
            own_doc = jnp.where(z == k, ends[k - 1], own_doc)
        pdoc[...] = jnp.broadcast_to(own_doc, pdoc.shape)
        p_in[z] = p_out[z]
        for k in range(1, n_z):
            z2 = lax.rem(z + k, n_z)
            send(p_out.at[z2], p_in.at[z], p_snd.at[k - 1], st_sem.at[z], {"z": z2})

    def carry_over():
        for k in range(1, n_z):
            z2 = lax.rem(z + k, n_z)
            landed(p_in.at[z2], st_sem.at[z2])
        opened = (dcol[...][:, :1] == pdoc[0:1, 0:1]).astype(F32)
        squares = jnp.zeros((toks, 128), F32)
        for h in range(2):
            rows = slice(32 * h, 32 * h + 32)
            state = jnp.concatenate([p_in[q, rows, :] for q in range(4)], axis=0)
            query = wq[pl.ds(h, toks, stride=2), :].astype(BF16)
            factor = jnp.exp(ccol[...][:, h : h + 1]) * opened
            mixed = mix[h] + dot_nn(query, state) * factor
            mix[h] = mixed
            squares = squares + mixed * mixed
        sums = dot_nt(jnp.ones((8, 128), F32), squares, precision=lax.Precision.HIGHEST)
        ss_in[tp] = sums[0:1, :]

    def post_squares():
        @pl.when(own_turn < n_tp - 1)
        def _():
            pl.semaphore_wait(ready, n_tp - 1 - own_turn)

        def post(k, carry):
            send(ss_in.at[tp], ss_in.at[tp], ss_snd.at[k], ss_sem.at[tp], tp_place(k))
            return carry

        lax.fori_loop(1, n_tp, post, 0)

    def finish_lin():
        def arrive(k, carry):
            t2 = lax.rem(tp + k, n_tp)
            landed(ss_in.at[t2], ss_sem.at[t2])
            return carry

        lax.fori_loop(1, n_tp, arrive, 0)
        total = jnp.sum(ss_in[...], axis=0)
        inv = lax.rsqrt(total / (n_tp * 2 * HEAD_DIM) + 1e-06)
        inv_col = as_column(inv, toks)
        for h in range(2):
            wo[pl.ds(h, toks, stride=2), :] = mix[h] * inv_col
        lin_out[...] = wo[...].astype(BF16)

    def order(it):
        return jnp.where(it == 4, 5, jnp.where(it == 5, 4, it))

    @pl.when(y == 0)
    def _():
        row_prefixes()

    for j in range(2):
        primary(0, j)

    def row_sent(it, carry):
        d = order(it)

        @pl.when(d <= y)
        def _():
            for j in range(2):
                zz = place(half, j)

                @pl.when((y + 1 < n_y) & (d + 1 < BACK))
                def _():
                    left(kv.at[c, 0], a_snd.at[2 * d + j])

                @pl.when((y + BACK < n_y) & (d == 0) & (zz >= z))
                def _():
                    left(kv.at[c, 0], a5_snd.at[j])

                @pl.when(seen_here(d, zz))
                def _():
                    left(kv.at[c, 0], x_snd.at[2 * d + j])

            for zz in range(4):

                @pl.when(seen_here(d, zz))
                def _():
                    left(kv.at[c, 0], b_snd.at[4 * d + zz])

        return carry

    def step(it, carry):
        past, now, after = (order(it - 1), order(it), order(it + 1))
        has_past = (it >= 1) & (past <= y)
        @pl.when(late & (it == 1))
        def _():
            carry_over()

        @pl.when(late & (it == 1))
        def _():
            post_squares()

        for j in range(2):

            @pl.when((it < BACK) & (after <= y))
            def _(j=j):
                primary(after, j)

            if j == 0:

                @pl.when(late & (it == 0) & (y > 0))
                def _():
                    row_prefixes()

                @pl.when(has_past)
                def _():
                    complete(past)

            else:

                @pl.when((it <= BACK) & (now <= y))
                def _():
                    secondary(now)

                @pl.when(jnp.logical_not(late) & (it == 0) & (y > 0))
                def _():
                    row_prefixes()

                @pl.when(jnp.logical_not(late) & (it == 1))
                def _():
                    carry_over()

                @pl.when(jnp.logical_not(late) & (it == 4))
                def _():
                    post_squares()

            @pl.when(has_past & (past == 0))
            def _(j=j):
                attend(past, j, True)

            @pl.when(has_past & (past > 0))
            def _(j=j):
                attend(past, j, False)

        @pl.when(it == BACK - 1)
        def _():
            for h in range(2):
                gate = wg[pl.ds(h, toks, stride=2), :]
                mix[h] = mix[h] * gain[h : h + 1, :] * jax.nn.sigmoid(gate)

        @pl.when(it == BACK)
        def _():
            lax.fori_loop(0, BACK, row_sent, 0)

        return carry

    lax.fori_loop(0, BACK + 2, step, 0)
    soft_out[...] = (acc[...] / l_scr[...]).astype(BF16)

    for k in range(n_z - 1):
        left(s_out.at[0], s_snd.at[k])
        left(p_out.at[0], p_snd.at[k])

        @pl.when(owner)
        def _():
            left(kv.at[c, z], za_snd.at[k])

    for d in range(1, BACK + 1):

        @pl.when(y + d < n_y)
        def _(d=d):
            left(t_out, t_snd.at[d])

    def sent(k, carry):
        left(ss_in.at[tp], ss_snd.at[k])
        return carry

    lax.fori_loop(1, n_tp, sent, 0)

    row_sent(BACK, 0)
    finish_lin()


def hand_over(lin, soft, lin_out, soft_out, sem):
    copies = [
        pltpu.make_async_copy(lin, lin_out, sem.at[0]),
        pltpu.make_async_copy(soft, soft_out, sem.at[1]),
    ]
    for copy in copies:
        copy.start()
    for copy in copies:
        copy.wait()


def body(sizes, lin_query, lin_key, lin_value, lin_gate, log_decay, norm_gain, doc_ids,
         soft_query, soft_key, soft_value):
    toks = lin_query.shape[0]
    n_tp = sizes[2] * sizes[3] * sizes[4]
    flat = lambda a: a.reshape(-1, HEAD_DIM)
    dma = pltpu.SemaphoreType.DMA
    rows = BACK + 1
    in_vmem = pl.BlockSpec(memory_space=pltpu.VMEM)
    in_place = pl.BlockSpec(memory_space=pl.ANY)
    lin_out, soft_out = pl.pallas_call(
        functools.partial(kernel, sizes),
        out_shape=(
            pltpu.VMEM((2 * toks, HEAD_DIM), BF16),
            pltpu.VMEM((2 * toks, HEAD_DIM), BF16),
        ),
        in_specs=[in_place] * 10,
        out_specs=(in_vmem, in_vmem),
        scratch_shapes=[
            pltpu.VMEM((2 * toks, 128), BF16),
            pltpu.VMEM((2 * toks, 128), BF16),
            pltpu.VMEM((2 * toks, 128), BF16),
            pltpu.VMEM((2 * toks, 128), BF16),
            pltpu.VMEM((2, toks), F32),
            pltpu.VMEM((2, 128), F32),
            pltpu.VMEM((1, toks), jnp.int32),
            pltpu.VMEM((2 * toks, 128), BF16),
            pltpu.VMEM((KV_HEADS * toks, 128), BF16),
            pltpu.VMEM((KV_HEADS * toks, 128), BF16),
            dma((10,)),
            pltpu.VMEM((2, 4 * rows, toks, 128), BF16),
            pltpu.VMEM((2, KV_HEADS * toks, 128), F32),
            pltpu.VMEM((2 * toks, 128), F32),
            pltpu.VMEM((2 * toks, 128), F32),
            pltpu.VMEM((2 * toks, 128), F32),
            pltpu.VMEM((2 * toks, 128), F32),
            pltpu.VMEM((2 * toks, 128), F32),
            pltpu.VMEM((8, toks), F32),
            pltpu.VMEM((toks, 8), F32),
            pltpu.VMEM((toks, 128), F32),
            pltpu.VMEM((2 * toks, 128), F32),
            pltpu.VMEM((2, toks, 128), F32),
            pltpu.VMEM((4, 80, 128), BF16),
            pltpu.VMEM((4, 80, 128), BF16),
            pltpu.VMEM((80, 128), BF16),
            pltpu.VMEM((rows, 80, 128), BF16),
            pltpu.VMEM((4, 64, 128), BF16),
            pltpu.VMEM((4, 64, 128), BF16),
            pltpu.VMEM((64, 128), F32),
            pltpu.VMEM((1, 128), F32),
            pltpu.VMEM((1, 128), F32),
            pltpu.VMEM((n_tp, 1, toks), F32),
            pltpu.VMEM((2 * toks, 128), F32),
            pltpu.VMEM((2 * toks, 128), F32),
            pltpu.VMEM((2 * toks, 128), F32),
            dma((2 * rows,)),
            dma((2 * rows,)),
            dma((4 * rows,)),
            dma((4,)),
            dma((rows,)),
            dma((4,)),
            dma((n_tp,)),
            pltpu.SemaphoreType.REGULAR,
            dma((3,)),
            dma((2 * rows,)),
            dma((2,)),
            dma((4 * rows,)),
            dma((2 * rows,)),
            dma((3,)),
            dma((rows,)),
            dma((3,)),
            dma((n_tp,)),
        ],
        compiler_params=pltpu.CompilerParams(
            collective_id=0, has_side_effects=True, vmem_limit_bytes=56 * 1024 * 1024
        ),
    )(
        flat(lin_query),
        flat(lin_key),
        flat(lin_value),
        flat(lin_gate),
        jnp.transpose(log_decay),
        norm_gain,
        doc_ids.reshape(1, toks),
        flat(soft_query),
        flat(soft_key),
        flat(soft_value),
    )
    lin_out, soft_out = pl.pallas_call(
        hand_over,
        out_shape=(
            jax.ShapeDtypeStruct((2 * toks, HEAD_DIM), BF16),
            jax.ShapeDtypeStruct((2 * toks, HEAD_DIM), BF16),
        ),
        in_specs=[in_vmem] * 2,
        out_specs=(in_place, in_place),
        scratch_shapes=[dma((2,))],
        compiler_params=pltpu.CompilerParams(vmem_limit_bytes=8 * 1024 * 1024),
    )(lin_out, soft_out)
    return lin_out.reshape(toks, 2, HEAD_DIM), soft_out.reshape(toks, 2, HEAD_DIM)


def solution(mesh, sizes=(8, 4, 2, 8, 2)):
    split = Mesh(mesh.devices.reshape(sizes), ("y", "z", "w", "x", "c"))
    placed = (
        P(SEQ, TP, None),
        P(SEQ, TP, None),
        P(SEQ, TP, None),
        P(SEQ, TP, None),
        P(SEQ, TP),
        P(TP, None),
        P(SEQ),
        P(SEQ, TP, None),
        P(SEQ, None, None),
        P(SEQ, None, None),
    )
    return jax.shard_map(
        functools.partial(body, sizes),
        mesh=split,
        in_specs=placed,
        out_specs=(P(SEQ, TP, None), P(SEQ, TP, None)),
        check_vma=False,
    )
```

```python
import functools
import math

import jax
import jax.numpy as jnp
from jax import lax
from jax.experimental import pallas as pl
from jax.experimental.pallas import tpu as pltpu
from jax.sharding import Mesh
from jax.sharding import PartitionSpec as P

HEADS = 64
HEAD_DIM = 128
KV_HEADS = 8
SEQ = ("y", "z")
TP = ("w", "x", "c")
MESH = pl.DeviceIdType.MESH
F32 = jnp.float32
BF16 = jnp.bfloat16
BACK = 5
DOCS = 4
LOW = -1e30


def dot_nt(a, b, **kw):
    return lax.dot_general(a, b, (((1,), (1,)), ((), ())), preferred_element_type=F32, **kw)


def dot_tn(a, b):
    return lax.dot_general(a, b, (((0,), (0,)), ((), ())), preferred_element_type=F32)


def dot_nn(a, b):
    return lax.dot_general(a, b, (((1,), (0,)), ((), ())), preferred_element_type=F32)


def as_column(row, toks):
    return jnp.concatenate(
        [
            jnp.transpose(jnp.broadcast_to(row[:, k : k + 128], (128, 128)))
            for k in range(0, toks, 128)
        ],
        axis=0,
    )


def three_parts(line):
    high = line.astype(BF16)
    rest = line - high.astype(F32)
    middle = rest.astype(BF16)
    low = (rest - middle.astype(F32)).astype(BF16)
    row = lax.broadcasted_iota(jnp.int32, (16, 128), 0)
    parts = [jnp.broadcast_to(p.astype(F32), (16, 128)) for p in (high, middle, low)]
    return jnp.where(
        row == 0, parts[0], jnp.where(row == 1, parts[1], jnp.where(row == 2, parts[2], 0.0))
    ).astype(BF16)


def from_parts(tile):
    wide = tile.astype(F32)
    return wide[0:1] + wide[1:2] + wide[2:3]


def kernel(
    sizes,
    lq_in,
    lk_in,
    lv_in,
    lg_in,
    ld_in,
    gain_in,
    docs_in,
    sq_in,
    sk_in,
    sv_in,
    lin_out,
    soft_out,
    lq,
    lk,
    lv,
    lg,
    ld,
    gain,
    docs,
    sq,
    sk,
    sv,
    in_sem,
    kv,
    wide8,
    wq,
    wk,
    wv,
    wg,
    wo,
    dec,
    ccol,
    dcol,
    dq,
    mix,
    s_out,
    s_in,
    t_out,
    t_in,
    p_out,
    p_in,
    run_state,
    run_decay,
    pdoc,
    ss_in,
    m_scr,
    l_scr,
    acc,
    p_sem,
    x_sem,
    c_sem,
    s_sem,
    t_sem,
    st_sem,
    ss_sem,
    ready,
    za_snd,
    a_snd,
    a5_snd,
    b_snd,
    x_snd,
    s_snd,
    t_snd,
    p_snd,
    ss_snd,
):
    n_y, n_z, n_w, n_x, n_c = sizes
    n_tp = n_w * n_x * n_c
    toks = docs.shape[1]
    y, z, w = (lax.axis_index("y"), lax.axis_index("z"), lax.axis_index("w"))
    x, c = (lax.axis_index("x"), lax.axis_index("c"))
    tp = (w * n_x + x) * n_c + c
    half = lax.rem(x, 2)
    other_half = 1 - half
    x_mate = x + 1 - 2 * half
    c_mate = 1 - c
    head = (tp * 2) // (HEADS // KV_HEADS)

    n_xc = n_x * n_c

    def tp_place(k):
        away = k <= n_tp - n_xc
        w2 = lax.rem(w + jnp.where(away, 1, 0), n_w)
        xc2 = lax.rem(x * n_c + c + k - jnp.where(away, 1, n_tp - n_xc), n_xc)
        return {"w": w2, "x": xc2 // n_c, "c": lax.rem(xc2, n_c)}

    def turn(w_, x_, c_):
        apart = jnp.minimum(x_, n_x - x_)
        step = 2 * apart - jnp.where((x_ >= 1) & (2 * x_ <= n_x), 1, 0)
        return (w_ * n_x + step) * n_c + c_

    own_turn = turn(w, x, c)
    barrier = pltpu.get_barrier_semaphore()

    def at_turn(t):
        step = lax.rem(t, n_xc) // n_c
        x2 = jnp.where(lax.rem(step, 2) == 1, (step + 1) // 2, n_x - step // 2)
        return {"w": t // n_xc, "x": lax.rem(x2, n_x), "c": lax.rem(t, n_c)}

    def greet_tp(t, carry):
        pl.semaphore_signal(barrier, inc=1, device_id=at_turn(t), device_id_type=MESH)
        return carry

    def tell_tp(t, carry):
        pl.semaphore_signal(ready, inc=1, device_id=at_turn(t), device_id_type=MESH)
        return carry

    def greet_y(k, carry):
        pl.semaphore_signal(
            barrier, inc=1, device_id={"y": lax.rem(y + k, n_y)}, device_id_type=MESH
        )
        return carry

    loads = [
        pltpu.make_async_copy(source, target, in_sem.at[k])
        for k, (source, target) in enumerate(
            (
                (docs_in, docs),
                (ld_in, ld),
                (lk_in, lk),
                (lv_in, lv),
                (sk_in, sk),
                (sv_in, sv),
                (lq_in, lq),
                (lg_in, lg),
                (sq_in, sq),
                (gain_in, gain),
            )
        )
    ]
    for load in loads:
        load.start()
    for k in range(1, n_z):
        pl.semaphore_signal(
            barrier, inc=1, device_id={"z": lax.rem(z + k, n_z)}, device_id_type=MESH
        )
    lax.fori_loop(1, n_y, greet_y, 0)

    @pl.when(c == 1)
    def _():
        pl.semaphore_signal(barrier, inc=1, device_id={"c": c_mate}, device_id_type=MESH)

    @pl.when(turn(w, x_mate, c) < own_turn)
    def _():
        pl.semaphore_signal(barrier, inc=1, device_id={"x": x_mate}, device_id_type=MESH)

    lax.fori_loop(own_turn + 1, n_tp, greet_tp, 0)

    def send(src, dst, send_sem, recv_sem, device):
        pltpu.make_async_remote_copy(
            src_ref=src,
            dst_ref=dst,
            send_sem=send_sem,
            recv_sem=recv_sem,
            device_id=device,
            device_id_type=MESH,
        ).start()

    def landed(ref, sem):
        pltpu.make_async_remote_copy(
            src_ref=ref,
            dst_ref=ref,
            send_sem=a5_snd.at[0],
            recv_sem=sem,
            device_id={"c": c_mate},
            device_id_type=MESH,
        ).wait_recv()

    def left(ref, sem):
        pltpu.make_async_remote_copy(
            src_ref=ref,
            dst_ref=ref,
            send_sem=sem,
            recv_sem=p_sem.at[0],
            device_id={"c": c_mate},
            device_id_type=MESH,
        ).wait_send()

    for load in loads[:4]:
        load.wait()
    doc_row = docs[...].astype(F32)
    doc_col = as_column(doc_row, toks)
    for source, target in ((lk, wk), (lv, wv)):
        target[...] = source[...].astype(F32)

    dec[...] = jnp.zeros_like(dec)
    dec[0:2, :] = ld[...]
    t_id = lax.broadcasted_iota(jnp.int32, (toks, toks), 0)
    s_id = lax.broadcasted_iota(jnp.int32, (toks, toks), 1)
    upto = (s_id <= t_id).astype(F32)
    cum_col = dot_nt(upto, dec[...], precision=lax.Precision.HIGHEST)
    cum_row = dot_nt(dec[...], upto, precision=lax.Precision.HIGHEST)
    ccol[...] = cum_col
    last_doc = doc_row[:, toks - 1 : toks]
    tail = (doc_col[:, :1] == last_doc).astype(F32)
    keys = [wk[pl.ds(h, toks, stride=2), :] for h in range(2)]
    values = [wv[pl.ds(h, toks, stride=2), :].astype(BF16) for h in range(2)]
    decay_line = jnp.zeros((1, 128), F32)
    lane = lax.broadcasted_iota(jnp.int32, (1, 128), 1)
    for h in range(2):
        end = cum_col[toks - 1 : toks, h : h + 1]
        scale = jnp.exp(end - cum_col[:, h : h + 1]) * tail
        state = dot_tn((keys[h] * scale).astype(BF16), values[h]).astype(BF16)
        for q in range(4):
            s_out[q, 32 * h : 32 * h + 32, :] = state[32 * q : 32 * q + 32, :]
        decay_line = jnp.where(lane == h, end, decay_line)
    decay_line = jnp.where(lane == 2, last_doc, decay_line)
    for v in range(DOCS):
        count = jnp.sum((doc_row == v).astype(F32), axis=1, keepdims=True)
        decay_line = jnp.where(lane == 3 + v, count, decay_line)
    scalars = three_parts(decay_line)
    for q in range(4):
        s_out[q, 64:80, :] = scalars
    s_in[z] = s_out[z]
    early_mates = c + jnp.where(turn(w, x_mate, c) < own_turn, 1, 0)

    def greeted_and_sent():
        pl.semaphore_wait(barrier, (n_z - 1) + (n_y - 1) + 2 + own_turn - early_mates)

        for k in range(1, n_z):
            z2 = lax.rem(z + k, n_z)
            send(s_out.at[z2], s_in.at[z], s_snd.at[k - 1], s_sem.at[z], {"z": z2})

    late = w == 1

    @pl.when(late)
    def _():
        greeted_and_sent()

    for load in loads[4:6]:
        load.wait()
    for kind, source in ((0, sk), (1, sv)):
        wide8[kind] = source[...].astype(F32)
        kv[kind, z] = wide8[kind, pl.ds(head, toks, stride=KV_HEADS), :].astype(BF16)

    for zz in range(4):
        in_half = ((zz == 0) or (zz == 3)) == (half == 0)
        for kind in range(2):

            @pl.when((zz > z) & jnp.logical_not(in_half & (c == kind)))
            def _(zz=zz, kind=kind):
                kv[kind, zz] = jnp.zeros(kv.shape[2:], BF16)

            @pl.when((zz < z) & (y >= BACK))
            def _(zz=zz, kind=kind):
                kv[kind, 4 * BACK + zz] = jnp.zeros(kv.shape[2:], BF16)

    @pl.when(jnp.logical_not(late))
    def _():
        greeted_and_sent()

    owner = ((z == 0) | (z == 3)) == (half == 0)

    @pl.when(owner)
    def _():
        for k in range(1, n_z):
            z2 = lax.rem(z + jnp.where(z < 2, n_z - k, k), n_z)
            send(kv.at[c, z], kv.at[c, z], za_snd.at[k - 1], p_sem.at[z // 2], {"z": z2})

    lax.fori_loop(0, own_turn, tell_tp, 0)
    dcol[...] = doc_col
    for h in range(2):
        dq[pl.ds(h, toks, stride=2), :] = doc_col
    for load in loads[6:]:
        load.wait()
    for source, target in ((lq, wq), (lg, wg)):
        target[...] = source[...].astype(F32)
    queries = [wq[pl.ds(h, toks, stride=2), :].astype(BF16) for h in range(2)]
    visible = (s_id <= t_id) & (doc_row == doc_col[:, :1])
    for h in range(2):
        gap = cum_col[:, h : h + 1] - cum_row[h : h + 1, :]
        factor = jnp.where(visible, jnp.exp(jnp.where(visible, gap, 0.0)), 0.0)
        weights = (dot_nt(queries[h], keys[h].astype(BF16)) * factor).astype(BF16)
        mix[h] = dot_nn(weights, values[h])
    m_scr[...] = jnp.full_like(m_scr, LOW)
    l_scr[...] = jnp.zeros_like(l_scr)
    acc[...] = jnp.zeros_like(acc)

    for k in range(1, n_z):
        z2 = lax.rem(z + k, n_z)
        landed(s_in.at[z2], s_sem.at[z2])
    lines = [from_parts(s_in[k, 64:80, :]) for k in range(4)]
    ends = [line[:, 2:3] for line in lines]

    def weight_of(first, last, h, doc):
        total = jnp.zeros((1, 1), F32)
        for k in range(first, last + 1):
            total = total + lines[k][:, h : h + 1]
        return jnp.where(doc == ends[last], jnp.exp(total), 0.0)

    total_line = lines[0] + lines[1] + lines[2] + lines[3]
    for h in range(2):
        rows = slice(32 * h, 32 * h + 32)
        total = s_in[3, rows, :].astype(F32)
        for k in range(3):
            total = total + s_in[k, rows, :].astype(F32) * weight_of(k + 1, 3, h, ends[k])
        t_out[rows, :] = total.astype(BF16)
    t_out[64:80, :] = three_parts(jnp.where(lane == 2, ends[3], total_line))
    for d in range(1, BACK + 1):

        @pl.when(y + d < n_y)
        def _(d=d):
            send(t_out, t_in.at[d], t_snd.at[d], t_sem.at[d], {"y": y + d})

    def place(which, j):
        return which + j * (3 - 2 * which)

    def seen_here(d, zz):
        return jnp.logical_not(((d == 0) & (zz >= z)) | ((d == BACK) & (zz < z)))

    def primary(d, j):
        zz = place(half, j)
        unit = kv.at[c, 4 * d + zz]

        @pl.when(jnp.logical_not(((d == 0) & (zz == z)) | ((d == BACK) & (zz < z))))
        def _():
            landed(unit, p_sem.at[2 * d + j])

        @pl.when((y + 1 < n_y) & (d + 1 < BACK))
        def _():
            send(
                unit,
                kv.at[c, 4 * d + 4 + zz],
                a_snd.at[2 * d + j],
                p_sem.at[2 * d + 2 + j],
                {"y": lax.rem(y + 1, n_y)},
            )

        @pl.when((y + BACK < n_y) & (d == 0) & (zz >= z))
        def _():
            send(
                unit,
                kv.at[c, 4 * BACK + zz],
                a5_snd.at[j],
                p_sem.at[2 * BACK + j],
                {"y": lax.rem(y + BACK, n_y)},
            )

        @pl.when(seen_here(d, zz))
        def _():
            send(unit, unit, x_snd.at[2 * d + j], x_sem.at[2 * d + j], {"x": x_mate})
            send(unit, unit, b_snd.at[4 * d + zz], c_sem.at[4 * d + zz], {"c": c_mate})

    def secondary(d):
        for j in range(2):
            zz = place(other_half, j)
            unit = kv.at[c, 4 * d + zz]

            @pl.when(seen_here(d, zz))
            def _():
                landed(unit, x_sem.at[2 * d + j])
                send(unit, unit, b_snd.at[4 * d + zz], c_sem.at[4 * d + zz], {"c": c_mate})

    def complete(d, blocks):
        for zz in blocks:

            @pl.when(seen_here(d, zz))
            def _():
                landed(kv.at[c_mate, 4 * d + zz], c_sem.at[4 * d + zz])

    score_scale = HEAD_DIM ** (-0.5) * math.log2(math.e)
    rows_per = toks

    def attend(d, part, same_row, blocks):
        def chunk(i, carry):
            first = pl.multiple_of(i * rows_per, rows_per)
            rows = pl.ds(first, rows_per)
            query = sq[rows, :]
            key_id = lax.broadcasted_iota(jnp.int32, (rows_per, toks), 1)
            inside = key_id.astype(F32) - dq[rows, :][:, :1]
            line_id = lax.broadcasted_iota(jnp.int32, (rows_per, toks), 0) + first
            query_pos = lax.shift_right_logical(line_id, 1) + z * toks
            ahead = query_pos - key_id
            scores = []
            for zz in blocks:
                slot = 4 * d + zz
                seen = inside >= ((4 * d - zz) * toks).astype(F32)
                if same_row:
                    seen = seen & (ahead >= zz * toks)
                score = dot_nt(query, kv[0, slot])
                scores.append(jnp.where(seen, score, LOW))
            top = functools.reduce(jnp.maximum, scores)
            old_top = m_scr[rows, :][:, :1]
            new_top = jnp.maximum(old_top, jnp.max(top, axis=1, keepdims=True))
            shrink = jnp.exp2((old_top - new_top) * score_scale)
            exps = [jnp.exp2((score - new_top) * score_scale) for score in scores]
            added = jnp.sum(functools.reduce(jnp.add, exps), axis=1, keepdims=True)
            weighted = jnp.zeros((rows_per, HEAD_DIM), F32)
            for part_exp, zz in zip(exps, blocks):
                weighted = weighted + dot_nn(part_exp.astype(BF16), kv[1, 4 * d + zz])
            m_scr[rows, :] = jnp.broadcast_to(new_top, (rows_per, 128))
            l_scr[rows, :] = l_scr[rows, :] * shrink + added
            acc[rows, :] = acc[rows, :] * shrink + weighted
            return carry

        each = toks // rows_per
        lax.fori_loop(part * each, part * each + each, chunk, 0)

    def row_prefixes():
        run_state[...] = jnp.zeros_like(run_state)
        run_decay[...] = jnp.zeros_like(run_decay)
        pdoc[...] = jnp.full_like(pdoc, -1.0)
        for d in range(1, BACK + 1):

            @pl.when(y >= d)
            def _(d=d):
                landed(t_in.at[d], t_sem.at[d])
                line = from_parts(t_in[d, 64:80, :])
                end = line[:, 2:3]
                if d == 1:
                    pdoc[...] = jnp.broadcast_to(end, pdoc.shape)
                for h in range(2):
                    rows = slice(32 * h, 32 * h + 32)
                    passed = run_decay[0:1, h : h + 1]
                    keep = jnp.where(end == pdoc[0:1, 0:1], jnp.exp(passed), 0.0)
                    run_state[rows, :] = run_state[rows, :] + t_in[d, rows, :].astype(F32) * keep
                run_decay[...] = run_decay[...] + line

        before = pdoc[0:1, 0:1]
        for h in range(2):
            rows = slice(32 * h, 32 * h + 32)
            entry = run_state[rows, :]
            p_out[0, rows, :] = entry.astype(BF16)
            for k in range(1, 4):
                prior = entry * weight_of(0, k - 1, h, before)
                for j in range(k):
                    part = s_in[j, rows, :].astype(F32)
                    if j < k - 1:
                        part = part * weight_of(j + 1, k - 1, h, ends[j])
                    prior = prior + part
                p_out[k, rows, :] = prior.astype(BF16)
        began = jnp.zeros((1, 1), F32)
        starts = jnp.zeros(dq.shape, F32)
        for v in range(DOCS):
            earlier = run_decay[0:1, 3 + v : 4 + v]
            first = jnp.where(earlier > 0, -earlier, began)
            starts = jnp.where(dq[...] == v, first, starts)
            began = began + total_line[:, 3 + v : 4 + v]
        dq[...] = starts
        own_doc = before
        for k in range(1, 4):
            own_doc = jnp.where(z == k, ends[k - 1], own_doc)
        pdoc[...] = jnp.broadcast_to(own_doc, pdoc.shape)
        p_in[z] = p_out[z]
        for k in range(1, n_z):
            z2 = lax.rem(z + k, n_z)
            send(p_out.at[z2], p_in.at[z], p_snd.at[k - 1], st_sem.at[z], {"z": z2})

    def carry_over():
        for k in range(1, n_z):
            z2 = lax.rem(z + k, n_z)
            landed(p_in.at[z2], st_sem.at[z2])
        opened = (dcol[...][:, :1] == pdoc[0:1, 0:1]).astype(F32)
        squares = jnp.zeros((toks, 128), F32)
        for h in range(2):
            rows = slice(32 * h, 32 * h + 32)
            state = jnp.concatenate([p_in[q, rows, :] for q in range(4)], axis=0)
            query = wq[pl.ds(h, toks, stride=2), :].astype(BF16)
            factor = jnp.exp(ccol[...][:, h : h + 1]) * opened
            mixed = mix[h] + dot_nn(query, state) * factor
            mix[h] = mixed
            squares = squares + mixed * mixed
        sums = dot_nt(jnp.ones((8, 128), F32), squares, precision=lax.Precision.HIGHEST)
        ss_in[tp] = sums[0:1, :]

    def post_squares():
        @pl.when(own_turn < n_tp - 1)
        def _():
            pl.semaphore_wait(ready, n_tp - 1 - own_turn)

        def post(k, carry):
            send(ss_in.at[tp], ss_in.at[tp], ss_snd.at[k], ss_sem.at[tp], tp_place(k))
            return carry

        lax.fori_loop(1, n_tp, post, 0)

    def finish_lin():
        def arrive(k, carry):
            t2 = lax.rem(tp + k, n_tp)
            landed(ss_in.at[t2], ss_sem.at[t2])
            return carry

        lax.fori_loop(1, n_tp, arrive, 0)
        total = jnp.sum(ss_in[...], axis=0)
        inv = lax.rsqrt(total / (n_tp * 2 * HEAD_DIM) + 1e-06)
        inv_col = as_column(inv, toks)
        for h in range(2):
            wo[pl.ds(h, toks, stride=2), :] = mix[h] * inv_col
        lin_out[...] = wo[...].astype(BF16)

    def order(it):
        return jnp.where(it == 4, 5, jnp.where(it == 5, 4, it))

    @pl.when(y == 0)
    def _():
        row_prefixes()

    for j in range(2):
        primary(0, j)

    def row_sent(it, carry):
        d = order(it)

        @pl.when(d <= y)
        def _():
            for j in range(2):
                zz = place(half, j)

                @pl.when((y + 1 < n_y) & (d + 1 < BACK))
                def _():
                    left(kv.at[c, 0], a_snd.at[2 * d + j])

                @pl.when((y + BACK < n_y) & (d == 0) & (zz >= z))
                def _():
                    left(kv.at[c, 0], a5_snd.at[j])

                @pl.when(seen_here(d, zz))
                def _():
                    left(kv.at[c, 0], x_snd.at[2 * d + j])

            for zz in range(4):

                @pl.when(seen_here(d, zz))
                def _():
                    left(kv.at[c, 0], b_snd.at[4 * d + zz])

        return carry

    def step(it, carry):
        past, now, after = (order(it - 1), order(it), order(it + 1))
        has_past = (it >= 1) & (past <= y)
        @pl.when(late & (it == 0) & (y > 0))
        def _():
            row_prefixes()

        @pl.when(late & (it == 1))
        def _():
            carry_over()

        @pl.when(late & (it == 1))
        def _():
            post_squares()

        for j in range(2):

            @pl.when((it < BACK) & (after <= y))
            def _(j=j):
                primary(after, j)

            if j == 0:

                @pl.when(has_past & (it <= BACK))
                def _():
                    complete(past, range(4))

                @pl.when(has_past & (it > BACK))
                def _():
                    complete(past, [place(other_half, k) for k in range(2)])

            else:

                @pl.when((it == BACK) & (now <= y))
                def _():
                    own = [place(half, k) for k in range(2)]
                    complete(now, own)
                    for part in range(2):
                        attend(now, part, False, own)

                @pl.when((it <= BACK) & (now <= y))
                def _():
                    secondary(now)

                @pl.when(jnp.logical_not(late) & (it == 0) & (y > 0))
                def _():
                    row_prefixes()

                @pl.when(jnp.logical_not(late) & (it == 1))
                def _():
                    carry_over()

                @pl.when(jnp.logical_not(late) & (it == 4))
                def _():
                    post_squares()

            @pl.when(has_past & (past == 0))
            def _(j=j):
                attend(past, j, True, range(4))

            @pl.when(has_past & (past > 0) & (it <= BACK))
            def _(j=j):
                attend(past, j, False, range(4))

            @pl.when(has_past & (it > BACK))
            def _(j=j):
                attend(past, j, False, [place(other_half, k) for k in range(2)])

        @pl.when(it == BACK - 1)
        def _():
            for h in range(2):
                gate = wg[pl.ds(h, toks, stride=2), :]
                mix[h] = mix[h] * gain[h : h + 1, :] * jax.nn.sigmoid(gate)

        @pl.when(it == BACK)
        def _():
            lax.fori_loop(0, BACK, row_sent, 0)

        return carry

    lax.fori_loop(0, BACK + 2, step, 0)
    soft_out[...] = (acc[...] / l_scr[...]).astype(BF16)

    for k in range(n_z - 1):
        left(s_out.at[0], s_snd.at[k])
        left(p_out.at[0], p_snd.at[k])

        @pl.when(owner)
        def _():
            left(kv.at[c, z], za_snd.at[k])

    for d in range(1, BACK + 1):

        @pl.when(y + d < n_y)
        def _(d=d):
            left(t_out, t_snd.at[d])

    def sent(k, carry):
        left(ss_in.at[tp], ss_snd.at[k])
        return carry

    lax.fori_loop(1, n_tp, sent, 0)

    row_sent(BACK, 0)
    finish_lin()


def hand_over(lin, soft, lin_out, soft_out, sem):
    copies = [
        pltpu.make_async_copy(lin, lin_out, sem.at[0]),
        pltpu.make_async_copy(soft, soft_out, sem.at[1]),
    ]
    for copy in copies:
        copy.start()
    for copy in copies:
        copy.wait()


def body(sizes, lin_query, lin_key, lin_value, lin_gate, log_decay, norm_gain, doc_ids,
         soft_query, soft_key, soft_value):
    toks = lin_query.shape[0]
    n_tp = sizes[2] * sizes[3] * sizes[4]
    flat = lambda a: a.reshape(-1, HEAD_DIM)
    dma = pltpu.SemaphoreType.DMA
    rows = BACK + 1
    in_vmem = pl.BlockSpec(memory_space=pltpu.VMEM)
    in_place = pl.BlockSpec(memory_space=pl.ANY)
    lin_out, soft_out = pl.pallas_call(
        functools.partial(kernel, sizes),
        out_shape=(
            pltpu.VMEM((2 * toks, HEAD_DIM), BF16),
            pltpu.VMEM((2 * toks, HEAD_DIM), BF16),
        ),
        in_specs=[in_place] * 10,
        out_specs=(in_vmem, in_vmem),
        scratch_shapes=[
            pltpu.VMEM((2 * toks, 128), BF16),
            pltpu.VMEM((2 * toks, 128), BF16),
            pltpu.VMEM((2 * toks, 128), BF16),
            pltpu.VMEM((2 * toks, 128), BF16),
            pltpu.VMEM((2, toks), F32),
            pltpu.VMEM((2, 128), F32),
            pltpu.VMEM((1, toks), jnp.int32),
            pltpu.VMEM((2 * toks, 128), BF16),
            pltpu.VMEM((KV_HEADS * toks, 128), BF16),
            pltpu.VMEM((KV_HEADS * toks, 128), BF16),
            dma((10,)),
            pltpu.VMEM((2, 4 * rows, toks, 128), BF16),
            pltpu.VMEM((2, KV_HEADS * toks, 128), F32),
            pltpu.VMEM((2 * toks, 128), F32),
            pltpu.VMEM((2 * toks, 128), F32),
            pltpu.VMEM((2 * toks, 128), F32),
            pltpu.VMEM((2 * toks, 128), F32),
            pltpu.VMEM((2 * toks, 128), F32),
            pltpu.VMEM((8, toks), F32),
            pltpu.VMEM((toks, 8), F32),
            pltpu.VMEM((toks, 128), F32),
            pltpu.VMEM((2 * toks, 128), F32),
            pltpu.VMEM((2, toks, 128), F32),
            pltpu.VMEM((4, 80, 128), BF16),
            pltpu.VMEM((4, 80, 128), BF16),
            pltpu.VMEM((80, 128), BF16),
            pltpu.VMEM((rows, 80, 128), BF16),
            pltpu.VMEM((4, 64, 128), BF16),
            pltpu.VMEM((4, 64, 128), BF16),
            pltpu.VMEM((64, 128), F32),
            pltpu.VMEM((1, 128), F32),
            pltpu.VMEM((1, 128), F32),
            pltpu.VMEM((n_tp, 1, toks), F32),
            pltpu.VMEM((2 * toks, 128), F32),
            pltpu.VMEM((2 * toks, 128), F32),
            pltpu.VMEM((2 * toks, 128), F32),
            dma((2 * rows,)),
            dma((2 * rows,)),
            dma((4 * rows,)),
            dma((4,)),
            dma((rows,)),
            dma((4,)),
            dma((n_tp,)),
            pltpu.SemaphoreType.REGULAR,
            dma((3,)),
            dma((2 * rows,)),
            dma((2,)),
            dma((4 * rows,)),
            dma((2 * rows,)),
            dma((3,)),
            dma((rows,)),
            dma((3,)),
            dma((n_tp,)),
        ],
        compiler_params=pltpu.CompilerParams(
            collective_id=0, has_side_effects=True, vmem_limit_bytes=56 * 1024 * 1024
        ),
    )(
        flat(lin_query),
        flat(lin_key),
        flat(lin_value),
        flat(lin_gate),
        jnp.transpose(log_decay),
        norm_gain,
        doc_ids.reshape(1, toks),
        flat(soft_query),
        flat(soft_key),
        flat(soft_value),
    )
    lin_out, soft_out = pl.pallas_call(
        hand_over,
        out_shape=(
            jax.ShapeDtypeStruct((2 * toks, HEAD_DIM), BF16),
            jax.ShapeDtypeStruct((2 * toks, HEAD_DIM), BF16),
        ),
        in_specs=[in_vmem] * 2,
        out_specs=(in_place, in_place),
        scratch_shapes=[dma((2,))],
        compiler_params=pltpu.CompilerParams(vmem_limit_bytes=8 * 1024 * 1024),
    )(lin_out, soft_out)
    return lin_out.reshape(toks, 2, HEAD_DIM), soft_out.reshape(toks, 2, HEAD_DIM)


def solution(mesh, sizes=(8, 4, 2, 8, 2)):
    split = Mesh(mesh.devices.reshape(sizes), ("y", "z", "w", "x", "c"))
    placed = (
        P(SEQ, TP, None),
        P(SEQ, TP, None),
        P(SEQ, TP, None),
        P(SEQ, TP, None),
        P(SEQ, TP),
        P(TP, None),
        P(SEQ),
        P(SEQ, TP, None),
        P(SEQ, None, None),
        P(SEQ, None, None),
    )
    return jax.shard_map(
        functools.partial(body, sizes),
        mesh=split,
        in_specs=placed,
        out_specs=(P(SEQ, TP, None), P(SEQ, TP, None)),
        check_vma=False,
    )
```
